32 devices in a mesh: groups: 2 (over x), tok: 16 (over z, y, core).
Axes of the slice: x: 2, y: 2, z: 4, core: 2. Of those that a mesh axis runs over, the one named last changes fastest.
Arguments:
- tokens: bfloat16 [8192, 1024], P(('groups', 'tok')), parts along dimension 0, may hold values from -6 to 6
- norm_gain: float32 [1024], replicated, may hold values from 0.1 to 1.9
- w_qk: bfloat16 [1024, 1024], replicated, may hold values from -0.1875 to 0.1875
- w_v: bfloat16 [1024, 1024], replicated, may hold values from -0.1875 to 0.1875
- cotangent: bfloat16 [8192, 1024], P(('groups', 'tok')), parts along dimension 0, may hold values from -48 to 48
- log_sums: float32 [2, 8, 8192], P(None, None, ('groups', 'tok')), parts along dimension 2, may hold values from 7 to 8
- bucket_order: int32 [2, 8192], P(None, 'groups'), parts along dimension 1, may hold values from 0 to 4095, as said below
- token_position: int32 [2, 8192], P(None, ('groups', 'tok')), parts along dimension 1, may hold values from 0 to 4095, as said below
Outputs:
- d_tokens: bfloat16 [8192, 1024], P(('groups', 'tok')), parts along dimension 0
- d_gain: float32 [2048], P(('groups', 'tok')), parts along dimension 0
- d_wqk: float32 [2048, 1024], P(('groups', 'tok')), parts along dimension 0
- d_wv: float32 [2048, 1024], P(('groups', 'tok')), parts along dimension 0
The draws below stay inside these ranges and needn't reach their ends.
There are 2 independent parts, one for each index of `groups`. The reference program is written for one: setup_inputs(seed, part) draws one part's arguments, and reference() takes and returns one part's arrays. A program takes and returns all parts, laid end to end along the dimension named above; an argument that names none is the same for every part. Nothing has to cross between parts.
Inputs may be any that keep to these rules, and one draw needn't show every extreme that they name: `bucket_order`: each row is a permutation; the 256 hash-sorted positions of one device hold at most 20 tokens of any one device's 256 tokens, and exactly 20 of at least one. token_position[r, bucket_order[r, p]] = p.
All inputs are finite; a program needn't handle non-finite values.
Results may differ from the reference program's by a relative error of at most 0.025.
Values may be sent and summed in bfloat16 or wider, within the bound.
A program may use at most 128 MiB of HBM per device.

```python
import math
import jax
import jax.numpy as jnp
from jax import lax

H = 8
DH = 128
D = 1024
BLOCK = 256
ROUNDS = 2
TOK_DEV = 256
TOKENS = 4096
CAP = 20
N_TOK = 16


def build_orderings(key):
    orderings = []
    for hashing in range(ROUNDS):
        round_key = jax.random.fold_in(key, 7001 + hashing)
        device_key, jitter_key, source_key, target_key, tie_key = jax.random.split(round_key, 5)
        spare_rows = TOK_DEV - CAP
        base_load = spare_rows // (N_TOK - 1)
        extra_rows = spare_rows % (N_TOK - 1)
        placed = jax.random.permutation(device_key, N_TOK).astype(jnp.int32)
        jitter = jax.random.randint(jitter_key, (N_TOK - 1,), 0, base_load // 4 + 1).astype(jnp.int32)
        weights = base_load + (jnp.arange(N_TOK - 1) < extra_rows).astype(jnp.int32) + jitter - jnp.roll(jitter, -1)
        weights = jnp.concatenate([jnp.array([CAP], jnp.int32), weights.astype(jnp.int32)])
        source_ids = jnp.broadcast_to(jnp.arange(N_TOK, dtype=jnp.int32)[:, None], (N_TOK, N_TOK))
        offsets = jnp.broadcast_to(jnp.arange(N_TOK, dtype=jnp.int32)[None, :], (N_TOK, N_TOK))
        target = placed[(source_ids + offsets) % N_TOK]
        pair_loads = jnp.zeros((N_TOK, N_TOK), jnp.int32).at[source_ids, target].set(jnp.broadcast_to(weights[None, :], (N_TOK, N_TOK)))

        def spread(row_load, subkey):
            listed = jnp.repeat(jnp.arange(N_TOK, dtype=jnp.int32), row_load, total_repeat_length=TOK_DEV)
            return jax.random.permutation(subkey, listed)
        token_dest = jax.vmap(spread)(pair_loads, jax.random.split(source_key, N_TOK)).reshape(-1).astype(jnp.int32)
        slot_source = jax.vmap(spread)(pair_loads.T, jax.random.split(target_key, N_TOK)).reshape(-1).astype(jnp.int32)
        tiebreak = jax.random.permutation(tie_key, TOKENS).astype(jnp.int32)
        block_ids = (jnp.arange(TOKENS, dtype=jnp.int32) // TOK_DEV).astype(jnp.int32)
        token_score = (token_dest * N_TOK + block_ids) * TOKENS + tiebreak
        place_score = (block_ids * N_TOK + slot_source) * TOKENS + jnp.arange(TOKENS, dtype=jnp.int32)
        token_sorted = jnp.argsort(token_score, stable=True).astype(jnp.int32)
        place_sorted = jnp.argsort(place_score, stable=True).astype(jnp.int32)
        ordering = jnp.zeros((TOKENS,), jnp.int32).at[place_sorted].set(token_sorted)
        orderings.append(ordering)
    return jnp.stack(orderings)


def draw_bucket_order(key, part):
    return build_orderings(key)


def draw_token_position(key, part):
    orderings = build_orderings(key)
    places = jnp.arange(TOKENS, dtype=jnp.int32)
    return jnp.stack([jnp.zeros((TOKENS,), jnp.int32).at[orderings[hashing]].set(places) for hashing in range(ROUNDS)])


def spiked(drawn, stream_key, source, target, blocks, factor):
    owner, partner = [(jnp.arange(drawn.shape[position]) // (drawn.shape[position] // blocks)).reshape([-1 if axis == position else 1 for axis in range(drawn.ndim)]) for position in (source, target)]
    chosen = jax.random.permutation(stream_key, blocks)[partner]
    strong = (owner == chosen) | (owner == (partner + blocks // 2) % blocks)
    return jnp.where(strong, factor * drawn, drawn)


def shard_levels(rng, extent, cuts, least, largest):
    factor_of = 1.0
    for dim, parts in cuts:
        steps = jax.random.uniform(jax.random.fold_in(jax.random.fold_in(rng, 6), dim), (parts,), jnp.float32, least / len(cuts), largest / len(cuts))
        factor_of = factor_of * jnp.repeat(jnp.exp(steps), extent[dim] // parts).reshape((-1,) + (1,) * (len(extent) - 1 - dim))
    return factor_of


def scatter_about(key, shape, width, reach, cuts=(), held_as=jnp.bfloat16):
    values = jax.random.normal(key, shape, jnp.float32) * width
    if len(cuts) > 0:
        values = shard_levels(key, shape, cuts, -0.22, 0.18) * values
    return jnp.clip(values, min=-reach, max=reach).astype(held_as)


def noise_with(own_key, shape, deviation, reach, cuts, heavy, held_as=jnp.bfloat16):
    drawn = deviation * jax.random.normal(own_key, shape, jnp.float32)
    if cuts:
        drawn = drawn * shard_levels(own_key, shape, cuts, -0.22, 0.18)
    return jnp.clip(spiked(drawn, jax.random.fold_in(own_key, 3), *heavy), -reach, reach).astype(held_as)


def setup_inputs(seed: int = 0, part: int = 0) -> dict:
    key_of = jax.random.split(jax.random.key(seed), 9)
    own_keys = jax.random.split(jax.random.fold_in(key_of[8], part), 9)
    return {
        "tokens": noise_with(own_keys[0], (TOKENS, D), 1.0, 6.0, ((0, 16),), (0, 1, 16, 2.0)),
        "norm_gain": jnp.clip(1.0 + 0.18 * jax.random.normal(key_of[1], (D,), jnp.float32), 0.1, 1.9),
        "w_qk": scatter_about(key_of[2], (D, D), D ** -0.5, 0.1875),
        "w_v": scatter_about(key_of[3], (D, D), D ** -0.5, 0.1875),
        "cotangent": scatter_about(own_keys[4], (TOKENS, D), 8.0, 48.0, ((0, 16),)),
        "log_sums": jnp.clip(7.0 + 1.0 * jax.random.uniform(own_keys[5], (ROUNDS, H, TOKENS), jnp.float32) ** shard_levels(own_keys[5], (ROUNDS, H, TOKENS), ((2, 16),), -0.2, 0.2), 7.0, 8.0),
        "bucket_order": draw_bucket_order(jax.random.fold_in(jax.random.fold_in(key_of[8], part), 71), part),
        "token_position": draw_token_position(jax.random.fold_in(jax.random.fold_in(key_of[8], part), 71), part),
    }


def normed(values, scales):
    return values * lax.rsqrt(lax.optimization_barrier(jnp.mean(values * values, axis=-1, keepdims=True)) + 1e-06) * scales

def unit_keys(queries):
    head_depth = queries.shape[-1]
    return queries * lax.rsqrt(lax.optimization_barrier(jnp.mean(queries * queries, axis=-1, keepdims=True)) + 1e-06) / math.sqrt(head_depth)

def attend(queries, keys_all, values_all, out_grads, log_sum):
    block_len = queries.shape[1]
    queries_f = queries.astype(jnp.float32)
    keys_f = keys_all.astype(jnp.float32)
    values_f = values_all.astype(jnp.float32)
    grads_f = out_grads.astype(jnp.float32)
    scores = jnp.einsum('cihe,cjhe->chij', queries_f, keys_f)
    diagonal = jnp.arange(2 * block_len)[None, :] == jnp.arange(block_len)[:, None] + block_len
    weights = jnp.where(diagonal, 0.0, jnp.exp(scores - log_sum[:, :, :, None]))
    d_weights = jnp.einsum('cihe,cjhe->chij', grads_f, values_f)
    totals = lax.optimization_barrier(jnp.sum(weights * d_weights, axis=-1, keepdims=True))
    d_scores = (weights * (d_weights - totals)).astype(jnp.bfloat16).astype(jnp.float32)
    weights_low = weights.astype(jnp.bfloat16).astype(jnp.float32)
    d_values = jnp.einsum('chij,cihe->cjhe', weights_low, grads_f)
    d_queries = jnp.einsum('chij,cjhe->cihe', d_scores, keys_f)
    d_keys = jnp.einsum('chij,cihe->cjhe', d_scores, queries_f)
    return (d_queries, d_keys, d_values)

def one_block(members):
    results = attend(*[member[None] for member in members])
    return tuple((result[0] for result in results))

def reference(tokens, norm_gain, w_qk, w_v, cotangent, log_sums, bucket_order, token_position):
    tokens_wide = tokens.astype(jnp.float32)
    normal_rows = normed(tokens_wide, norm_gain).astype(jnp.bfloat16)
    query_rows = jnp.dot(normal_rows, w_qk, preferred_element_type=jnp.float32).astype(jnp.bfloat16)
    value_rows = jnp.dot(normal_rows, w_v, preferred_element_type=jnp.float32).astype(jnp.bfloat16)
    block_count = TOKENS // BLOCK
    d_normal = jnp.zeros((TOKENS, D), jnp.float32)
    grad_qk = jnp.zeros((D, D), jnp.float32)
    grad_v = jnp.zeros((D, D), jnp.float32)
    for hashing in range(ROUNDS):
        order_row = bucket_order[hashing]
        query_four = query_rows[order_row].reshape(block_count, BLOCK, H, DH)
        value_four = value_rows[order_row].reshape(block_count, BLOCK, H, DH)
        grad_four = cotangent[order_row].reshape(block_count, BLOCK, H, DH)
        unit_four = unit_keys(query_four.astype(jnp.float32)).astype(jnp.bfloat16)
        block_sums = log_sums[hashing].reshape(H, block_count, BLOCK).transpose(1, 0, 2)
        keys_all = jnp.concatenate([jnp.roll(unit_four, 1, axis=0), unit_four], axis=1)
        values_all = jnp.concatenate([jnp.roll(value_four, 1, axis=0), value_four], axis=1)
        d_query, d_keys, d_values = lax.map(one_block, (query_four, keys_all, values_all, grad_four, block_sums))
        key_grad = d_keys[:, BLOCK:] + jnp.roll(d_keys[:, :BLOCK], -1, axis=0)
        value_grad = d_values[:, BLOCK:] + jnp.roll(d_values[:, :BLOCK], -1, axis=0)
        _, key_pull = jax.vjp(unit_keys, query_four.astype(jnp.float32))
        query_grad = d_query + key_pull(key_grad)[0]
        places = token_position[hashing]
        query_low = query_grad.reshape(TOKENS, D).astype(jnp.bfloat16)[places]
        value_low = value_grad.reshape(TOKENS, D).astype(jnp.bfloat16)[places]
        grad_qk = grad_qk + jnp.dot(normal_rows.T, query_low, preferred_element_type=jnp.float32)
        grad_v = grad_v + jnp.dot(normal_rows.T, value_low, preferred_element_type=jnp.float32)
        d_normal = d_normal + jnp.dot(query_low, w_qk.T, preferred_element_type=jnp.float32) + jnp.dot(value_low, w_v.T, preferred_element_type=jnp.float32)
    _, norm_pull = jax.vjp(normed, tokens_wide, norm_gain)
    d_tokens, grad_gain = norm_pull(d_normal)
    grad_scale = 1.0 / math.sqrt(TOKENS)
    return (d_tokens.astype(jnp.bfloat16), grad_gain * grad_scale, grad_qk * grad_scale, grad_v * grad_scale)
```

```python
import functools
import math

import jax
import jax.numpy as jnp
from jax import lax
from jax.experimental import pallas as pl
from jax.experimental.pallas import tpu as pltpu
from jax.sharding import PartitionSpec as P

BLOCK = 256
EPS = 1e-06
VMEM_LIMIT = 63 * 1024 * 1024
MESH = pl.DeviceIdType.MESH
F32 = jnp.float32
BF16 = jnp.bfloat16


def whole(count):
    return [pl.BlockSpec(memory_space=pltpu.VMEM)] * count


def dot_nn(a, b):
    return lax.dot_general(a, b, (((1,), (0,)), ((), ())), preferred_element_type=F32)


def dot_nt(a, b):
    return lax.dot_general(a, b, (((1,), (1,)), ((), ())), preferred_element_type=F32)


def dot_tn(a, b):
    return lax.dot_general(a, b, (((0,), (0,)), ((), ())), preferred_element_type=F32)


def slot_row(order, tok_dev, stride):
    size = order.shape[1]
    owner = lax.div(order, jnp.int32(tok_dev))
    owner_col = jnp.broadcast_to(owner, (size, size)).T
    before = lax.broadcasted_iota(jnp.int32, (size, size), 0) < lax.broadcasted_iota(
        jnp.int32, (size, size), 1
    )
    earlier = (owner_col == owner) & before
    rank = jnp.sum(earlier.astype(F32), axis=0, keepdims=True).astype(jnp.int32)
    return owner * stride + rank


def one_hot_rows(slots, slot_count):
    size = slots.shape[1]
    ids = lax.broadcasted_iota(jnp.int32, (slot_count, size), 0)
    return jnp.where(ids == slots, 1.0, 0.0).astype(BF16)


def normal_of(x, gain):
    return (x * lax.rsqrt(jnp.mean(x * x, axis=-1, keepdims=True) + EPS) * gain).astype(BF16)


def unit_of(q):
    depth = q.shape[-1]
    scale = lax.rsqrt(jnp.mean(q * q, axis=-1, keepdims=True) + EPS)
    return (q * scale / math.sqrt(depth)).astype(BF16)


def flipped(index, mask):
    bit = 1
    while bit <= mask:
        if mask & bit:
            index = index + bit * (1 - 2 * lax.rem(lax.div(index, bit), 2))
        bit *= 2
    return index


def forwarding_order(masks):
    return sorted(masks, key=lambda m: int(bin(m)[:1:-1].ljust(16, "0"), 2), reverse=True)


def core_kernel(heads, stride, split, grad_scale, *refs):
    gain_ref, order_ref, sums_ref, tokens_ref, cot_ref, qk_ref, v_ref = refs[:7]
    d_tokens_ref, d_gain_ref, d_qk_ref, d_v_ref = refs[7:11]
    (
        normal, slab_out, slab_in, sums_out, sums_in_rows, spread, pick, bucket, back_bucket,
        sorted_q, sorted_k, sorted_g, sorted_v, probs, d_key, d_query,
        part_out, part_in, home_out, home_in, grads,
        gain_out, gain_back, weights, sums_in, sums_run,
        slab_sem, relay_sem, rows_sem, part_sem, home_sem, gain_sem, sums_sem,
    ) = refs[11:]
    devices = lax.axis_size("tok")
    me = lax.axis_index("tok")
    rounds, seq_len = order_ref.shape
    rows, width = tokens_ref.shape
    depth = width // heads
    chips = devices // rounds
    chip, lane = lax.div(me, rounds), lax.rem(me, rounds)
    blocks = seq_len // rows
    queries = blocks // split
    first = lax.rem(chip, split) * queries
    held = range(1 if split == 1 else 0, queries + 1)
    held_count = len(held)
    slot_count = devices * stride
    parts = [slice(head * depth, (head + 1) * depth) for head in range(heads)]

    def remote(src, dst, sems, peer):
        return pltpu.make_async_remote_copy(
            src_ref=src,
            dst_ref=dst,
            send_sem=sems.at[0],
            recv_sem=sems.at[1],
            device_id={"tok": peer},
            device_id_type=MESH,
        )

    barrier = pltpu.get_barrier_semaphore()
    for step in range(1, devices):
        peer = lax.rem(me + step, devices)
        pl.semaphore_signal(barrier, inc=1, device_id={"tok": peer}, device_id_type=MESH)

    def chip_at(step):
        return lax.rem(chip + step, chips)

    def chip_behind(step):
        return lax.rem(chip + chips - step, chips)

    def lane_at(step):
        return lax.rem(lane + step, rounds)

    def lane_behind(step):
        return lax.rem(lane + rounds - step, rounds)

    slabs = [
        {
            step: remote(
                slab_out.at[t, lax.div(chip_at(step), split)],
                slab_in.at[t, lane, chip],
                slab_sem.at[t, step - 1],
                chip_at(step) * rounds + lane,
            )
            for step in range(1, chips)
        }
        for t in range(3)
    ]
    relays = [
        {
            (d, step): remote(
                slab_in.at[t, lane, chip_behind(step)],
                slab_in.at[t, lane, chip_behind(step)],
                relay_sem.at[t, d - 1, step],
                chip * rounds + lane_at(d),
            )
            for d in range(1, rounds)
            for step in range(chips)
        }
        for t in range(3)
    ]
    row_sums = []
    for step in range(1, devices):
        peer = lax.rem(me + step, devices)
        unit = lax.div(lax.div(peer, rounds), split) * rounds + lax.rem(peer, rounds)
        row_sums.append(remote(sums_out.at[unit], sums_in_rows.at[me], rows_sem.at[step - 1], peer))
    shares = [
        {
            (d, step): remote(
                part_out.at[t, d - 1, step],
                part_in.at[t, d - 1, step],
                part_sem.at[t, d - 1, step],
                chip * rounds + lane_at(d),
            )
            for d in range(1, rounds)
            for step in range(chips)
        }
        for t in range(2)
    ]
    homes = [
        {
            step: remote(
                home_out.at[t, step],
                home_in.at[t, chip],
                home_sem.at[t, step - 1],
                chip_at(step) * rounds + lane,
            )
            for step in range(1, chips)
        }
        for t in range(2)
    ]
    gains = []
    for step in range(1, devices):
        peer = lax.rem(me + step, devices)
        gains.append(remote(gain_out.at[peer], gain_back.at[me], gain_sem.at[step - 1], peer))

    bits = devices.bit_length() - 1
    first_slot = [devices - (devices >> k) for k in range(bits)]

    def sums_copy(half, k, mask):
        slot = first_slot[k] + (mask >> (k + 1))
        source = weights.at[half, flipped(me, mask)] if k == 0 else sums_run.at[half, mask >> 1]
        return remote(
            source, sums_in.at[half, slot], sums_sem.at[half, slot], flipped(me, 1 << k)
        )

    stages = [
        [{m: sums_copy(half, k, m) for m in range(1 << k, devices, 2 << k)} for half in range(2)]
        for k in range(bits)
    ]
    far_first = sorted(range(1, chips), key=lambda step: -min(step, chips - step))

    def send_slabs(t):
        for step in far_first:
            slabs[t][step].start()
        slab_in[t, lane, chip] = slab_out[t, lax.div(chip, split)]

    normal[...] = normal_of(tokens_ref[...].astype(F32), gain_ref[...])
    query = dot_nn(normal[...], qk_ref[...]).astype(BF16)
    for head, part in enumerate(parts):
        slab_out[0, head] = query[:, part]
    for hashing in range(rounds):
        for head in range(heads):
            sums_out[head * rounds + hashing] = sums_ref[hashing, head : head + 1, :]
    pl.semaphore_wait(barrier, devices - 1)
    send_slabs(0)
    own_unit = lax.div(chip, split) * rounds + lane
    sums_in_rows[me] = sums_out[own_unit]
    for copy in row_sums:
        copy.start()
    for head, part in enumerate(parts):
        slab_out[1, head] = cot_ref[:, part]
    send_slabs(1)
    value = dot_nn(normal[...], v_ref[...]).astype(BF16)
    for head, part in enumerate(parts):
        slab_out[2, head] = value[:, part]
    send_slabs(2)
    for t in range(3):
        for d in range(1, rounds):
            relays[t][d, 0].start()

    token_ids = lax.broadcasted_iota(jnp.int32, (rows, rows), 0)
    for place, j in enumerate(held):
        block = lax.rem(first + (j - 1 + blocks), blocks)
        start = pl.multiple_of(block * rows, rows)
        order = order_ref[pl.ds(lane, 1), pl.ds(start, rows)]
        chosen = one_hot_rows(slot_row(order, rows, stride), slot_count)
        pick[place] = chosen
        within = jnp.where(token_ids == lax.rem(order, jnp.int32(rows)), 1.0, 0.0).astype(BF16)
        moved = dot_nt(chosen, within).astype(BF16)
        spread[:, place] = moved.reshape(devices, stride, rows)

    def bucket_rows(t, source_chip, source_lane):
        source = source_chip * rounds + source_lane
        table = spread[source].reshape(held_count * stride, rows)
        placed = dot_nn(table, slab_in[t, source_lane, source_chip]).astype(BF16)
        bucket[source] = placed.reshape(held_count, stride, depth)

    arrival = [0, *sorted(range(1, chips), key=lambda step: min(step, chips - step))]

    def gather(t):
        for step in arrival:
            if step > 0:
                slabs[t][step].wait_recv()
                for d in range(1, rounds):
                    relays[t][d, step].start()
            bucket_rows(t, chip_behind(step), lane)
        for d in range(1, rounds):
            for step in arrival:
                relays[t][d, step].wait_recv()
                bucket_rows(t, chip_behind(step), lane_behind(d))

    def sorted_rows(place):
        data = bucket[:, place].reshape(slot_count, depth)
        return dot_tn(pick[place], data).astype(BF16)

    gather(0)
    for place, j in enumerate(held):
        q = sorted_rows(place)
        sorted_q[j] = q
        sorted_k[j] = unit_of(q.astype(F32))
    if split == 1:
        sorted_k[0] = sorted_k[queries]
    for copy in row_sums:
        copy.wait_recv()
    log_sums = sums_in_rows[pl.ds(first, queries)].reshape(queries, rows).T
    diagonal = lax.broadcasted_iota(jnp.int32, (rows, 2 * rows), 0) + rows == (
        lax.broadcasted_iota(jnp.int32, (rows, 2 * rows), 1)
    )
    for j in range(1, queries + 1):
        keys = sorted_k[j - 1 : j + 1].reshape(2 * rows, depth)
        scores = dot_nt(sorted_q[j], keys) - log_sums[:, j - 1 : j]
        probs[j] = jnp.where(diagonal, 0.0, jnp.exp(scores)).astype(BF16)

    def bucket_back(place, grad):
        placed = dot_nn(pick[place], grad).astype(BF16)
        back_bucket[:, place] = placed.reshape(devices, stride, depth)

    def home_rows(source_chip, source_lane):
        source = source_chip * rounds + source_lane
        table = spread[source].reshape(held_count * stride, rows)
        return dot_tn(table, back_bucket[source].reshape(held_count * stride, depth))

    def send_home(t):
        for d in range(1, rounds):
            for step in [*far_first, 0]:
                part_out[t, d - 1, step] = home_rows(chip_at(step), lane_at(d)).astype(BF16)
                shares[t][d, step].start()
        for step in [*far_first, 0]:
            total = home_rows(chip_at(step), lane)
            for d in range(1, rounds):
                shares[t][d, step].wait_recv()
                total += part_in[t, d - 1, step].astype(F32)
            if step > 0:
                home_out[t, step] = total.astype(BF16)
                homes[t][step].start()
            else:
                home_in[t, chip] = total.astype(BF16)

    gather(1)
    for place, j in enumerate(held):
        sorted_g[j] = sorted_rows(place)
    for place, j in enumerate(held):
        grad = jnp.zeros((rows, depth), F32)
        if j > 0:
            grad += dot_tn(probs[j, :, rows:], sorted_g[j])
        after = j + 1 if j < queries else 1
        if after > 1 or split == 1 or j == 0:
            if j < queries or split == 1:
                grad += dot_tn(probs[after, :, :rows], sorted_g[after])
        bucket_back(place, grad.astype(BF16))
    send_home(0)

    gather(2)
    for place, j in enumerate(held):
        sorted_v[j] = sorted_rows(place)
    if split == 1:
        sorted_v[0] = sorted_v[queries]

    def pull_key(j):
        q = sorted_q[j].astype(F32)
        dk = d_key[j]
        scale = lax.rsqrt(jnp.mean(q * q, axis=-1, keepdims=True) + EPS)
        along = jnp.mean(q * dk, axis=-1, keepdims=True)
        pulled = (dk * scale - q * (scale * scale * scale * along)) / math.sqrt(depth)
        if j > 0:
            pulled += d_query[j]
        bucket_back(j - held[0], pulled.astype(BF16))

    for j in range(1, queries + 1):
        values = sorted_v[j - 1 : j + 1].reshape(2 * rows, depth)
        keys = sorted_k[j - 1 : j + 1].reshape(2 * rows, depth)
        w = probs[j].astype(F32)
        d_probs = dot_nt(sorted_g[j], values)
        delta = jnp.sum(w * d_probs, axis=-1, keepdims=True)
        d_scores = (w * (d_probs - delta)).astype(BF16)
        d_query[j] = dot_nn(d_scores, keys)
        both = dot_tn(d_scores, sorted_q[j])
        if j == 1:
            d_key[0] = both[:rows]
        else:
            d_key[j - 1] += both[:rows]
        d_key[j] = both[rows:]
        if j > 1:
            pull_key(j - 1)
    if split == 1:
        d_key[queries] += d_key[0]
    else:
        pull_key(0)
    pull_key(queries)
    send_home(1)

    def assemble(t):
        for step in range(1, chips):
            homes[t][step].wait_recv()
        for head, part in enumerate(parts):
            total = home_in[t, head * split]
            for p in range(1, split):
                total = (total.astype(F32) + home_in[t, head * split + p].astype(F32)).astype(BF16)
            grads[t, :, part] = total

    def weight_gradient(t, half):
        grad = (dot_tn(normal[...], grads[t]) * grad_scale).astype(BF16)
        weights[half] = grad.reshape(devices, width // devices, width)
        for mask in forwarding_order(stages[0][half]):
            stages[0][half][mask].start()

    assemble(0)
    weight_gradient(0, 1)
    d_normal = dot_nt(grads[0], v_ref[...])
    assemble(1)
    weight_gradient(1, 0)
    d_normal += dot_nt(grads[1], qk_ref[...])
    x = tokens_ref[...].astype(F32)
    scale = lax.rsqrt(jnp.mean(x * x, axis=-1, keepdims=True) + EPS)
    gain_total = jnp.sum(d_normal * (x * scale), axis=0, keepdims=True) * grad_scale
    share = width // devices
    gain_out[...] = jnp.zeros(gain_out.shape, F32)
    for device in range(devices):
        gain_out[device, 0:1, 0:share] = gain_total[:, device * share : (device + 1) * share]
    gain_back[me] = gain_out[me]
    for copy in gains:
        copy.start()
    t = d_normal * gain_ref[...]
    along = jnp.mean(x * t, axis=-1, keepdims=True)
    d_tokens_ref[...] = (t * scale - x * (scale * scale * scale * along)).astype(BF16)

    outs = (d_qk_ref, d_v_ref)
    for k in range(bits):
        waiting = None
        for half in (1, 0):
            for mask in forwarding_order(stages[k][half]):
                mine = mask - (1 << k)
                stages[k][half][mask].wait_recv()
                arrived_sum = sums_in[half, first_slot[k] + (mask >> (k + 1))].astype(F32)
                before = weights[half, flipped(me, mine)] if k == 0 else sums_run[half, mine >> 1]
                run = before.astype(F32) + arrived_sum
                if k == bits - 1:
                    outs[half][...] = run
                    continue
                sums_run[half, mine >> 1] = run.astype(BF16)
                if waiting is not None:
                    waiting.start()
                waiting = stages[k + 1][half].get(mine)
        if waiting is not None:
            waiting.start()
    for copy in gains:
        copy.wait_recv()
    d_gain_ref[...] = jnp.sum(gain_back[:, 0, :], axis=0, keepdims=True)
    for stage in stages:
        for copy in [*stage[0].values(), *stage[1].values()]:
            copy.wait_send()
    for group in [*slabs, *relays, *shares, *homes]:
        for copy in group.values():
            copy.wait_send()
    for copy in [*row_sums, *gains]:
        copy.wait_send()


def per_device(tokens, norm_gain, w_qk, w_v, cotangent, log_sums, bucket_order, token_position):
    devices = lax.axis_size("tok")
    tok_dev, width = tokens.shape
    rounds, seq_len = bucket_order.shape
    heads = log_sums.shape[1]
    units = rounds * heads
    assert tok_dev == BLOCK and devices % units == 0
    split = devices // units
    chips = devices // rounds
    depth = width // heads
    queries = seq_len // tok_dev // split
    held = queries if split == 1 else queries + 1
    capacity = 5 * tok_dev // (4 * devices)
    stride = -(-capacity // 8) * 8
    grad_scale = 1.0 / math.sqrt(seq_len)
    share = width // devices
    dma = pltpu.SemaphoreType.DMA

    def low(*shape):
        return pltpu.VMEM(shape, BF16)

    d_tokens, d_gain, d_qk, d_v = pl.pallas_call(
        functools.partial(core_kernel, heads, stride, split, grad_scale),
        out_shape=[
            jax.ShapeDtypeStruct((tok_dev, width), BF16),
            jax.ShapeDtypeStruct((1, 128), F32),
            jax.ShapeDtypeStruct((share, width), F32),
            jax.ShapeDtypeStruct((share, width), F32),
        ],
        in_specs=whole(7),
        out_specs=whole(4),
        scratch_shapes=[
            low(tok_dev, width),
            low(3, heads, tok_dev, depth),
            low(3, rounds, chips, tok_dev, depth),
            pltpu.VMEM((units, 1, tok_dev), F32),
            pltpu.VMEM((devices, 1, tok_dev), F32),
            low(devices, held, stride, tok_dev),
            low(held, devices * stride, tok_dev),
            low(devices, held, stride, depth),
            low(devices, held, stride, depth),
            *[low(queries + 1, tok_dev, depth)] * 4,
            low(queries + 1, tok_dev, 2 * tok_dev),
            *[pltpu.VMEM((queries + 1, tok_dev, depth), F32)] * 2,
            *[low(2, rounds - 1, chips, tok_dev, depth)] * 2,
            *[low(2, chips, tok_dev, depth)] * 2,
            low(2, tok_dev, width),
            *[pltpu.VMEM((devices, 8, 128), F32)] * 2,
            low(2, devices, share, width),
            low(2, devices - 1, share, width),
            low(2, devices // 2, share, width),
            dma((3, chips - 1, 2)),
            dma((3, rounds - 1, chips, 2)),
            dma((devices - 1, 2)),
            dma((2, rounds - 1, chips, 2)),
            dma((2, chips - 1, 2)),
            dma((devices - 1, 2)),
            dma((2, devices - 1, 2)),
        ],
        compiler_params=pltpu.CompilerParams(
            vmem_limit_bytes=VMEM_LIMIT, collective_id=0, has_side_effects=True
        ),
        name="core",
    )(norm_gain.reshape(1, width), bucket_order, log_sums, tokens, cotangent, w_qk, w_v)
    return (d_tokens, d_gain[0, :share], d_qk, d_v)


def solution(mesh):
    in_specs = (
        P(("groups", "tok"), None),
        P(),
        P(),
        P(),
        P(("groups", "tok"), None),
        P(None, None, ("groups", "tok")),
        P(None, "groups"),
        P(None, ("groups", "tok")),
    )
    out_specs = (
        P(("groups", "tok"), None),
        P(("groups", "tok")),
        P(("groups", "tok"), None),
        P(("groups", "tok"), None),
    )
    return jax.shard_map(
        per_device, mesh=mesh, in_specs=in_specs, out_specs=out_specs, check_vma=False
    )
```

```python
import functools
import math

import jax
import jax.numpy as jnp
from jax import lax
from jax.experimental import pallas as pl
from jax.experimental.pallas import tpu as pltpu
from jax.sharding import PartitionSpec as P

BLOCK = 256
EPS = 1e-06
VMEM_LIMIT = 63 * 1024 * 1024
MESH = pl.DeviceIdType.MESH
F32 = jnp.float32
BF16 = jnp.bfloat16


def whole(count):
    return [pl.BlockSpec(memory_space=pltpu.VMEM)] * count


def dot_nn(a, b):
    return lax.dot_general(a, b, (((1,), (0,)), ((), ())), preferred_element_type=F32)


def dot_nt(a, b):
    return lax.dot_general(a, b, (((1,), (1,)), ((), ())), preferred_element_type=F32)


def dot_tn(a, b):
    return lax.dot_general(a, b, (((0,), (0,)), ((), ())), preferred_element_type=F32)


def slot_row(order, tok_dev, stride):
    size = order.shape[1]
    owner = lax.div(order, jnp.int32(tok_dev))
    owner_col = jnp.broadcast_to(owner, (size, size)).T
    before = lax.broadcasted_iota(jnp.int32, (size, size), 0) < lax.broadcasted_iota(
        jnp.int32, (size, size), 1
    )
    earlier = (owner_col == owner) & before
    rank = jnp.sum(earlier.astype(F32), axis=0, keepdims=True).astype(jnp.int32)
    return owner * stride + rank


def one_hot_rows(slots, slot_count):
    size = slots.shape[1]
    ids = lax.broadcasted_iota(jnp.int32, (slot_count, size), 0)
    return jnp.where(ids == slots, 1.0, 0.0).astype(BF16)


def normal_of(x, gain):
    return (x * lax.rsqrt(jnp.mean(x * x, axis=-1, keepdims=True) + EPS) * gain).astype(BF16)


def unit_of(q):
    depth = q.shape[-1]
    scale = lax.rsqrt(jnp.mean(q * q, axis=-1, keepdims=True) + EPS)
    return (q * scale / math.sqrt(depth)).astype(BF16)


def flipped(index, mask):
    bit = 1
    while bit <= mask:
        if mask & bit:
            index = index + bit * (1 - 2 * lax.rem(lax.div(index, bit), 2))
        bit *= 2
    return index


def forwarding_order(masks):
    return sorted(masks, key=lambda m: int(bin(m)[:1:-1].ljust(16, "0"), 2), reverse=True)


def looped(count, unroll, body):
    steps = count // unroll

    def step(i, carry):
        for u in range(unroll):
            body(i * unroll + u)
        return carry

    if steps > 1:
        lax.fori_loop(0, steps, step, 0)
    for i in range(steps * unroll if steps > 1 else 0, count):
        body(i)


def core_kernel(heads, stride, split, grad_scale, *refs):
    gain_hbm, order_hbm, sums_hbm, tokens_hbm, cot_hbm, qk_hbm, v_hbm = refs[:7]
    d_tokens_ref, d_gain_ref, d_qk_ref, d_v_ref = refs[7:11]
    (
        gain_ref, order_ref, sums_ref, tokens_ref, cot_ref, qk_ref, v_ref,
        normal, slab_out, slab_in, sums_out, sums_in_rows, spread, pick, bucket,
        sorted_q, sorted_k, sorted_g, sorted_v, probs, key_own, key_before, d_query,
        part_out, part_in, home_out, home_in, grads,
        gain_out, gain_back, weights, sums_in, sums_run,
        load_sem, slab_sem, relay_sem, rows_sem, part_sem, home_sem, gain_sem, sums_sem,
    ) = refs[11:]
    devices = lax.axis_size("tok")
    me = lax.axis_index("tok")
    rounds, seq_len = order_ref.shape
    rows, width = tokens_ref.shape
    depth = width // heads
    chips = devices // rounds
    chip, lane = lax.div(me, rounds), lax.rem(me, rounds)
    blocks = seq_len // rows
    queries = blocks // split
    first = lax.rem(chip, split) * queries
    base = 1 if split == 1 else 0
    held = queries + 1 - base
    slot_count = devices * stride
    parts = [slice(head * depth, (head + 1) * depth) for head in range(heads)]

    def remote(src, dst, sems, peer):
        return pltpu.make_async_remote_copy(
            src_ref=src,
            dst_ref=dst,
            send_sem=sems.at[0],
            recv_sem=sems.at[1],
            device_id={"tok": peer},
            device_id_type=MESH,
        )

    barrier = pltpu.get_barrier_semaphore()
    for step in range(1, devices):
        peer = lax.rem(me + step, devices)
        pl.semaphore_signal(barrier, inc=1, device_id={"tok": peer}, device_id_type=MESH)
    loads = {
        name: pltpu.make_async_copy(src, dst, load_sem.at[place])
        for place, (name, src, dst) in enumerate(
            [
                ("tokens", tokens_hbm, tokens_ref),
                ("gain", gain_hbm, gain_ref),
                ("qk", qk_hbm, qk_ref),
                ("sums", sums_hbm, sums_ref),
                ("cot", cot_hbm, cot_ref),
                ("order", order_hbm, order_ref),
                ("v", v_hbm, v_ref),
            ]
        )
    }
    for load in loads.values():
        load.start()

    def chip_at(step):
        return lax.rem(chip + step, chips)

    def chip_behind(step):
        return lax.rem(chip + chips - step, chips)

    def lane_at(step):
        return lax.rem(lane + step, rounds)

    def lane_behind(step):
        return lax.rem(lane + rounds - step, rounds)

    slabs = [
        {
            step: remote(
                slab_out.at[t, lax.div(chip_at(step), split)],
                slab_in.at[t, lane, chip],
                slab_sem.at[t, step - 1],
                chip_at(step) * rounds + lane,
            )
            for step in range(1, chips)
        }
        for t in range(3)
    ]
    relays = [
        {
            (d, step): remote(
                slab_in.at[t, lane, chip_behind(step)],
                slab_in.at[t, lane, chip_behind(step)],
                relay_sem.at[t, d - 1, step],
                chip * rounds + lane_at(d),
            )
            for d in range(1, rounds)
            for step in range(chips)
        }
        for t in range(3)
    ]
    row_sums = []
    for step in range(1, devices):
        peer = lax.rem(me + step, devices)
        unit = lax.div(lax.div(peer, rounds), split) * rounds + lax.rem(peer, rounds)
        row_sums.append(remote(sums_out.at[unit], sums_in_rows.at[me], rows_sem.at[step - 1], peer))
    shares = [
        {
            (d, step): remote(
                part_out.at[d - 1, step],
                part_in.at[t, d - 1, step],
                part_sem.at[t, d - 1, step],
                chip * rounds + lane_at(d),
            )
            for d in range(1, rounds)
            for step in range(chips)
        }
        for t in range(2)
    ]
    homes = [
        {
            step: remote(
                home_out.at[t, step],
                home_in.at[t, chip],
                home_sem.at[t, step - 1],
                chip_at(step) * rounds + lane,
            )
            for step in range(1, chips)
        }
        for t in range(2)
    ]
    gains = []
    for step in range(1, devices):
        peer = lax.rem(me + step, devices)
        gains.append(remote(gain_out.at[peer], gain_back.at[me], gain_sem.at[step - 1], peer))

    bits = devices.bit_length() - 1
    first_slot = [devices - (devices >> k) for k in range(bits)]
    bit_orders = [list(range(bits)), [0, *range(2, bits), 1]]
    streams = len(bit_orders)
    piece = width // streams

    def physical(stream, mask):
        return sum(1 << bit_orders[stream][k] for k in range(bits) if mask >> k & 1)

    def sums_copy(half, stream, k, mask):
        slot = first_slot[k] + (mask >> (k + 1))
        if k == 0:
            source = weights.at[half, stream, flipped(me, physical(stream, mask))]
        else:
            source = sums_run.at[half, stream, mask >> 1]
        peer = flipped(me, 1 << bit_orders[stream][k])
        return remote(
            source, sums_in.at[half, stream, slot], sums_sem.at[half, stream, slot], peer
        )

    stages = [
        [
            [
                {m: sums_copy(half, stream, k, m) for m in range(1 << k, devices, 2 << k)}
                for stream in range(streams)
            ]
            for half in range(2)
        ]
        for k in range(bits)
    ]
    far_first = sorted(range(1, chips), key=lambda step: -min(step, chips - step))
    near_first = far_first[::-1]

    def send_slabs(t):
        for step in far_first:
            slabs[t][step].start()
        slab_in[t, lane, chip] = slab_out[t, lax.div(chip, split)]

    with jax.named_scope("first"):
        loads["tokens"].wait()
        loads["gain"].wait()
        normal[...] = normal_of(tokens_ref[...].astype(F32), gain_ref[...])
        loads["qk"].wait()
        query = dot_nn(normal[...], qk_ref[...]).astype(BF16)
        for head, part in enumerate(parts):
            slab_out[0, head] = query[:, part]
        loads["sums"].wait()
        for hashing in range(rounds):
            for head in range(heads):
                sums_out[head * rounds + hashing] = sums_ref[hashing, head : head + 1, :]
        loads["cot"].wait()
        for head, part in enumerate(parts):
            slab_out[1, head] = cot_ref[:, part]
    with jax.named_scope("barrier"):
        pl.semaphore_wait(barrier, devices - 1)
    with jax.named_scope("sends"):
        for copy in row_sums:
            copy.start()
        send_slabs(0)
        own_unit = lax.div(chip, split) * rounds + lane
        sums_in_rows[me] = sums_out[own_unit]
        send_slabs(1)
        loads["v"].wait()
        value = dot_nn(normal[...], v_ref[...]).astype(BF16)
        for head, part in enumerate(parts):
            slab_out[2, head] = value[:, part]
        send_slabs(2)
        for t in range(3):
            for d in range(1, rounds):
                relays[t][d, 0].start()
        loads["order"].wait()

    token_ids = lax.broadcasted_iota(jnp.int32, (rows, rows), 0)

    def tables(place):
        block = lax.rem(first + (place + base - 1 + blocks), blocks)
        start = pl.multiple_of(block * rows, rows)
        order = order_ref[pl.ds(lane, 1), pl.ds(start, rows)]
        chosen = one_hot_rows(slot_row(order, rows, stride), slot_count)
        pick[place] = chosen
        within = jnp.where(token_ids == lax.rem(order, jnp.int32(rows)), 1.0, 0.0).astype(BF16)
        moved = dot_nt(chosen, within).astype(BF16)
        spread[:, place] = moved.reshape(devices, stride, rows)

    with jax.named_scope("tables"):
        looped(held, 4, tables)

    def bucket_rows(t, source_chip, source_lane):
        source = source_chip * rounds + source_lane
        table = spread[source].reshape(held * stride, rows)
        placed = dot_nn(table, slab_in[t, source_lane, source_chip]).astype(BF16)
        bucket[source] = placed.reshape(held, stride, depth)

    def take_slabs(t):
        with jax.named_scope(f"take{t}"):
            for step in near_first:
                slabs[t][step].wait_recv()
                for d in range(1, rounds):
                    relays[t][d, step].start()

    def gather(t):
        with jax.named_scope(f"gather{t}"):
            looped(chips, 8, lambda step: bucket_rows(t, chip_behind(step), lane))
            for d in range(1, rounds):
                for step in [0, *near_first]:
                    relays[t][d, step].wait_recv()
                looped(chips, 8, lambda step: bucket_rows(t, chip_behind(step), lane_behind(d)))

    def sorted_rows(place):
        data = bucket[:, place].reshape(slot_count, depth)
        return dot_tn(pick[place], data).astype(BF16)

    def sort_queries(place):
        q = sorted_rows(place)
        sorted_q[place + base] = q
        sorted_k[place + base] = unit_of(q.astype(F32))

    take_slabs(0)
    gather(0)
    with jax.named_scope("sortq"):
        looped(held, 4, sort_queries)
    if split == 1:
        sorted_k[0] = sorted_k[queries]
    with jax.named_scope("rowsums"):
        for copy in row_sums:
            copy.wait_recv()
    diagonal = lax.broadcasted_iota(jnp.int32, (2 * rows, rows), 0) == rows + (
        lax.broadcasted_iota(jnp.int32, (2 * rows, rows), 1)
    )

    def probabilities(i):
        keys = sorted_k[pl.ds(i, 2)].reshape(2 * rows, depth)
        scores = dot_nt(keys, sorted_q[i + 1]) - sums_in_rows[first + i]
        probs[i + 1] = jnp.where(diagonal, 0.0, jnp.exp(scores)).astype(BF16)

    with jax.named_scope("probs"):
        looped(queries, 4, probabilities)
    if split > 1:
        probs[0] = jnp.zeros((2 * rows, rows), BF16)
        probs[queries + 1] = jnp.zeros((2 * rows, rows), BF16)
        sorted_g[queries + 1] = jnp.zeros((rows, depth), BF16)

    def after(j):
        return lax.rem(j, queries) + 1 if split == 1 else j + 1

    def bucket_back(place, grad):
        placed = dot_nn(pick[place], grad).astype(BF16)
        bucket[:, place] = placed.reshape(devices, stride, depth)

    def home_rows(source_chip, source_lane):
        source = source_chip * rounds + source_lane
        table = spread[source].reshape(held * stride, rows)
        return dot_tn(table, bucket[source].reshape(held * stride, depth))

    def send_home(t):
        with jax.named_scope(f"home{t}"):
            if t > 0:
                for copy in shares[t - 1].values():
                    copy.wait_send()
            for d in range(1, rounds):

                def share(step):
                    part_out[d - 1, step] = home_rows(chip_at(step), lane_at(d)).astype(BF16)

                looped(chips, 8, share)
                for step in [*far_first, 0]:
                    shares[t][d, step].start()

            def keep(step):
                d_query[step] = home_rows(chip_at(step), lane)

            looped(chips, 8, keep)
            for step in [*far_first, 0]:
                for d in range(1, rounds):
                    shares[t][d, step].wait_recv()

            for step in [*far_first, 0]:
                total = d_query[step]
                for d in range(1, rounds):
                    total += part_in[t, d - 1, step].astype(F32)
                home_out[t, step] = total.astype(BF16)
            for step in far_first:
                homes[t][step].start()
            home_in[t, chip] = home_out[t, 0]

    take_slabs(1)
    gather(1)

    def sort_cotangents(place):
        sorted_g[place + base] = sorted_rows(place)

    def value_gradients(place):
        j = place + base
        grad = dot_nn(probs[j, rows:, :], sorted_g[j])
        grad += dot_nn(probs[after(j), :rows, :], sorted_g[after(j)])
        bucket_back(place, grad.astype(BF16))

    with jax.named_scope("sortg"):
        looped(held, 16, sort_cotangents)
    with jax.named_scope("dv"):
        looped(held, 16, value_gradients)
    send_home(0)
    take_slabs(2)
    gather(2)

    def sort_values(place):
        sorted_v[place + base] = sorted_rows(place)

    with jax.named_scope("sortv"):
        looped(held, 16, sort_values)
    if split == 1:
        sorted_v[0] = sorted_v[queries]
    else:
        key_own[0] = jnp.zeros((rows, depth), F32)
        d_query[0] = jnp.zeros((rows, depth), F32)
        key_before[queries + 1] = jnp.zeros((rows, depth), F32)

    def score_gradients(i):
        j = i + 1
        values = sorted_v[pl.ds(i, 2)].reshape(2 * rows, depth)
        keys = sorted_k[pl.ds(i, 2)].reshape(2 * rows, depth)
        w = probs[j].astype(F32)
        d_probs = dot_nt(values, sorted_g[j])
        delta = jnp.sum(w * d_probs, axis=0, keepdims=True)
        d_scores = (w * (d_probs - delta)).astype(BF16)
        d_query[j] = dot_tn(d_scores, keys)
        both = dot_nn(d_scores, sorted_q[j])
        key_before[j] = both[:rows]
        key_own[j] = both[rows:]

    def query_gradients(place):
        j = place + base
        q = sorted_q[j].astype(F32)
        dk = key_own[j] + key_before[after(j)]
        scale = lax.rsqrt(jnp.mean(q * q, axis=-1, keepdims=True) + EPS)
        along = jnp.mean(q * dk, axis=-1, keepdims=True)
        pulled = (dk * scale - q * (scale * scale * scale * along)) / math.sqrt(depth)
        bucket_back(place, (d_query[j] + pulled).astype(BF16))


    def assemble(t):
        with jax.named_scope(f"wait_home{t}"):
            for step in near_first:
                homes[t][step].wait_recv()
        for head, part in enumerate(parts):
            total = home_in[t, head * split]
            for p in range(1, split):
                total = (total.astype(F32) + home_in[t, head * split + p].astype(F32)).astype(BF16)
            grads[t, :, part] = total

    def weight_gradient(t, half):
        with jax.named_scope(f"weight{half}"):
            for stream in range(streams):
                columns = slice(stream * piece, (stream + 1) * piece)
                grad = (dot_tn(normal[...], grads[t, :, columns]) * grad_scale).astype(BF16)
                weights[half, stream] = grad.reshape(devices, width // devices, piece)
            for stream in range(streams):
                for mask in forwarding_order(stages[0][half][stream]):
                    stages[0][half][stream][mask].start()

    outs = (d_qk_ref, d_v_ref)

    def run_sums(k, halves):
        waiting = []
        with jax.named_scope(f"sum{k}_{halves[0]}"):
            for half in halves:
                for masks in zip(*[forwarding_order(stages[k][half][s]) for s in range(streams)]):
                    for stream, mask in enumerate(masks):
                        rest = mask - (1 << k)
                        stages[k][half][stream][mask].wait_recv()
                        slot = first_slot[k] + (mask >> (k + 1))
                        came = sums_in[half, stream, slot].astype(F32)
                        if k == 0:
                            before = weights[half, stream, flipped(me, physical(stream, rest))]
                        else:
                            before = sums_run[half, stream, rest >> 1]
                        run = before.astype(F32) + came
                        if k == bits - 1:
                            outs[half][:, stream * piece : (stream + 1) * piece] = run
                            continue
                        sums_run[half, stream, rest >> 1] = run.astype(BF16)
                        waiting.append(stages[k + 1][half][stream].get(rest))
                        if len(waiting) > 1:
                            onward = waiting.pop(0)
                            if onward is not None:
                                onward.start()
            for onward in waiting:
                if onward is not None:
                    onward.start()

    with jax.named_scope("ds"):
        looped(queries, 16, score_gradients)
    assemble(0)
    weight_gradient(0, 1)
    with jax.named_scope("dq"):
        looped(held, 16, query_gradients)
    run_sums(0, (1,))
    send_home(1)
    d_normal = dot_nt(grads[0], v_ref[...])
    run_sums(1, (1,))
    assemble(1)
    weight_gradient(1, 0)
    with jax.named_scope("rows"):
        d_normal += dot_nt(grads[1], qk_ref[...])
        x = tokens_ref[...].astype(F32)
        scale = lax.rsqrt(jnp.mean(x * x, axis=-1, keepdims=True) + EPS)
        gain_total = jnp.sum(d_normal * (x * scale), axis=0, keepdims=True) * grad_scale
        share = width // devices
        gain_out[...] = jnp.zeros(gain_out.shape, F32)
        for device in range(devices):
            gain_out[device, 0:1, 0:share] = gain_total[:, device * share : (device + 1) * share]
        gain_back[me] = gain_out[me]
        for copy in gains:
            copy.start()
        t = d_normal * gain_ref[...]
        along = jnp.mean(x * t, axis=-1, keepdims=True)
        d_tokens_ref[...] = (t * scale - x * (scale * scale * scale * along)).astype(BF16)

    run_sums(0, (0,))
    run_sums(2, (1,))
    run_sums(1, (0,))
    for k in range(2, bits):
        run_sums(k, (0,))
        if k + 1 < bits:
            run_sums(k + 1, (1,))
    with jax.named_scope("sendwaits"):
        for copy in gains:
            copy.wait_recv()
        d_gain_ref[...] = jnp.sum(gain_back[:, 0, :], axis=0, keepdims=True)
        for stage in stages:
            for half in stage:
                for stream in half:
                    for copy in stream.values():
                        copy.wait_send()
        for group in [*slabs, *relays, shares[-1], *homes]:
            for copy in group.values():
                copy.wait_send()
        for copy in [*row_sums, *gains]:
            copy.wait_send()


def hand_over(share, d_tokens_in, d_gain_in, d_qk_in, d_v_in, d_tokens, d_gain, d_qk, d_v):
    d_tokens[...] = d_tokens_in[...]
    d_gain[...] = d_gain_in[:, :share]
    d_qk[...] = d_qk_in[...]
    d_v[...] = d_v_in[...]


def per_device(tokens, norm_gain, w_qk, w_v, cotangent, log_sums, bucket_order, token_position):
    devices = lax.axis_size("tok")
    tok_dev, width = tokens.shape
    rounds, seq_len = bucket_order.shape
    heads = log_sums.shape[1]
    units = rounds * heads
    assert tok_dev == BLOCK and devices % units == 0
    split = devices // units
    chips = devices // rounds
    depth = width // heads
    queries = seq_len // tok_dev // split
    held = queries if split == 1 else queries + 1
    capacity = 5 * tok_dev // (4 * devices)
    stride = -(-capacity // 8) * 8
    grad_scale = 1.0 / math.sqrt(seq_len)
    share = width // devices
    dma = pltpu.SemaphoreType.DMA

    def low(*shape):
        return pltpu.VMEM(shape, BF16)

    def full(*shape):
        return pltpu.VMEM(shape, F32)

    results = pl.pallas_call(
        functools.partial(core_kernel, heads, stride, split, grad_scale),
        out_shape=[
            jax.ShapeDtypeStruct((tok_dev, width), BF16),
            jax.ShapeDtypeStruct((1, 128), F32),
            jax.ShapeDtypeStruct((share, width), F32),
            jax.ShapeDtypeStruct((share, width), F32),
        ],
        in_specs=[pl.BlockSpec(memory_space=pl.ANY)] * 7,
        out_specs=whole(4),
        scratch_shapes=[
            full(1, width),
            pltpu.VMEM((rounds, seq_len), jnp.int32),
            full(rounds, heads, tok_dev),
            low(tok_dev, width),
            low(tok_dev, width),
            low(width, width),
            low(width, width),
            low(tok_dev, width),
            low(3, heads, tok_dev, depth),
            low(3, rounds, chips, tok_dev, depth),
            full(units, 1, tok_dev),
            full(devices, 1, tok_dev),
            low(devices, held, stride, tok_dev),
            low(held, devices * stride, tok_dev),
            low(devices, held, stride, depth),
            *[low(queries + 2, tok_dev, depth)] * 4,
            low(queries + 2, 2 * tok_dev, tok_dev),
            *[full(queries + 2, tok_dev, depth)] * 3,
            low(rounds - 1, chips, tok_dev, depth),
            low(2, rounds - 1, chips, tok_dev, depth),
            *[low(2, chips, tok_dev, depth)] * 2,
            low(2, tok_dev, width),
            *[full(devices, 8, 128)] * 2,
            low(2, 2, devices, share, width // 2),
            low(2, 2, devices - 1, share, width // 2),
            low(2, 2, devices // 2, share, width // 2),
            dma((7,)),
            dma((3, chips - 1, 2)),
            dma((3, rounds - 1, chips, 2)),
            dma((devices - 1, 2)),
            dma((2, rounds - 1, chips, 2)),
            dma((2, chips - 1, 2)),
            dma((devices - 1, 2)),
            dma((2, 2, devices - 1, 2)),
        ],
        compiler_params=pltpu.CompilerParams(
            vmem_limit_bytes=VMEM_LIMIT, collective_id=0, has_side_effects=True
        ),
        name="core",
    )(norm_gain.reshape(1, width), bucket_order, log_sums, tokens, cotangent, w_qk, w_v)
    d_tokens, d_gain, d_qk, d_v = pl.pallas_call(
        functools.partial(hand_over, share),
        out_shape=[
            jax.ShapeDtypeStruct((tok_dev, width), BF16),
            jax.ShapeDtypeStruct((1, share), F32),
            jax.ShapeDtypeStruct((share, width), F32),
            jax.ShapeDtypeStruct((share, width), F32),
        ],
        in_specs=whole(4),
        out_specs=whole(4),
        name="hand_over",
    )(*results)
    return (d_tokens, d_gain.reshape(share), d_qk, d_v)


def solution(mesh):
    in_specs = (
        P(("groups", "tok"), None),
        P(),
        P(),
        P(),
        P(("groups", "tok"), None),
        P(None, None, ("groups", "tok")),
        P(None, "groups"),
        P(None, ("groups", "tok")),
    )
    out_specs = (
        P(("groups", "tok"), None),
        P(("groups", "tok")),
        P(("groups", "tok"), None),
        P(("groups", "tok"), None),
    )
    return jax.shard_map(
        per_device, mesh=mesh, in_specs=in_specs, out_specs=out_specs, check_vma=False
    )
```

```python
import functools
import math

import jax
import jax.numpy as jnp
from jax import lax
from jax.experimental import pallas as pl
from jax.experimental.pallas import tpu as pltpu
from jax.sharding import PartitionSpec as P

BLOCK = 256
EPS = 1e-06
VMEM_LIMIT = 63 * 1024 * 1024
MESH = pl.DeviceIdType.MESH
F32 = jnp.float32
BF16 = jnp.bfloat16


def whole(count):
    return [pl.BlockSpec(memory_space=pltpu.VMEM)] * count


def dot_nn(a, b):
    return lax.dot_general(a, b, (((1,), (0,)), ((), ())), preferred_element_type=F32)


def dot_nt(a, b):
    return lax.dot_general(a, b, (((1,), (1,)), ((), ())), preferred_element_type=F32)


def dot_tn(a, b):
    return lax.dot_general(a, b, (((0,), (0,)), ((), ())), preferred_element_type=F32)


def slot_row(order, tok_dev, stride):
    size = order.shape[1]
    owner = lax.div(order, jnp.int32(tok_dev))
    owner_col = jnp.broadcast_to(owner, (size, size)).T
    before = lax.broadcasted_iota(jnp.int32, (size, size), 0) < lax.broadcasted_iota(
        jnp.int32, (size, size), 1
    )
    earlier = (owner_col == owner) & before
    rank = jnp.sum(earlier.astype(F32), axis=0, keepdims=True).astype(jnp.int32)
    return owner * stride + rank


def one_hot_rows(slots, slot_count):
    size = slots.shape[1]
    ids = lax.broadcasted_iota(jnp.int32, (slot_count, size), 0)
    return jnp.where(ids == slots, 1.0, 0.0).astype(BF16)


def normal_of(x, gain):
    return (x * lax.rsqrt(jnp.mean(x * x, axis=-1, keepdims=True) + EPS) * gain).astype(BF16)


def unit_of(q):
    depth = q.shape[-1]
    scale = lax.rsqrt(jnp.mean(q * q, axis=-1, keepdims=True) + EPS)
    return (q * scale / math.sqrt(depth)).astype(BF16)


def flipped(index, mask):
    bit = 1
    while bit <= mask:
        if mask & bit:
            index = index + bit * (1 - 2 * lax.rem(lax.div(index, bit), 2))
        bit *= 2
    return index


def forwarding_order(masks):
    return sorted(masks, key=lambda m: int(bin(m)[:1:-1].ljust(16, "0"), 2), reverse=True)


def looped(count, unroll, body):
    steps = count // unroll

    def step(i, carry):
        for u in range(unroll):
            body(i * unroll + u)
        return carry

    if steps > 1:
        lax.fori_loop(0, steps, step, 0)
    for i in range(steps * unroll if steps > 1 else 0, count):
        body(i)


def core_kernel(heads, stride, split, grad_scale, *refs):
    gain_hbm, order_hbm, sums_hbm, tokens_hbm, cot_hbm, qk_hbm, v_hbm = refs[:7]
    d_tokens_ref, d_gain_ref, d_qk_ref, d_v_ref = refs[7:11]
    (
        gain_ref, order_ref, sums_ref, tokens_ref, qk_ref, v_ref,
        normal, slab_out, slab_in, sums_out, sums_in_rows, spread, pick, bucket,
        sorted_q, sorted_k, sorted_g, sorted_v, probs, d_query,
        part_out, part_in, home_out, home_in, grads,
        gain_out, gain_back, weights, sums_in, sums_run,
        cot_sem, load_sem, slab_sem, relay_sem, rows_sem, part_sem, home_sem, gain_sem, sums_sem,
    ) = refs[11:]
    devices = lax.axis_size("tok")
    me = lax.axis_index("tok")
    rounds, seq_len = order_ref.shape
    rows, width = tokens_ref.shape
    depth = width // heads
    chips = devices // rounds
    chip, lane = lax.div(me, rounds), lax.rem(me, rounds)
    blocks = seq_len // rows
    queries = blocks // split
    first = lax.rem(chip, split) * queries
    base = 1 if split == 1 else 0
    held = queries + 1 - base
    slot_count = devices * stride
    parts = [slice(head * depth, (head + 1) * depth) for head in range(heads)]

    def remote(src, dst, sems, peer):
        return pltpu.make_async_remote_copy(
            src_ref=src,
            dst_ref=dst,
            send_sem=sems.at[0],
            recv_sem=sems.at[1],
            device_id={"tok": peer},
            device_id_type=MESH,
        )

    barrier = pltpu.get_barrier_semaphore()
    for step in range(1, devices):
        peer = lax.rem(me + step, devices)
        pl.semaphore_signal(barrier, inc=1, device_id={"tok": peer}, device_id_type=MESH)
    cot_loads = [
        pltpu.make_async_copy(cot_hbm.at[:, part], slab_out.at[0, head], cot_sem.at[head])
        for head, part in enumerate(parts)
    ]
    loads = {
        name: pltpu.make_async_copy(src, dst, load_sem.at[place])
        for place, (name, src, dst) in enumerate(
            [
                ("sums", sums_hbm, sums_ref),
                ("tokens", tokens_hbm, tokens_ref),
                ("gain", gain_hbm, gain_ref),
                ("qk", qk_hbm, qk_ref),
                ("v", v_hbm, v_ref),
                ("order", order_hbm, order_ref),
            ]
        )
    }
    loads["sums"].start()
    for load in cot_loads:
        load.start()

    def chip_at(step):
        return flipped(chip, step)

    def lane_at(step):
        return lax.rem(lane + step, rounds)

    def lane_behind(step):
        return lax.rem(lane + rounds - step, rounds)

    slabs = [
        {
            step: remote(
                slab_out.at[t, lax.div(chip_at(step), split)],
                slab_in.at[t, lane, chip],
                slab_sem.at[t, step - 1],
                chip_at(step) * rounds + lane,
            )
            for step in range(1, chips)
        }
        for t in range(3)
    ]
    relays = [
        {
            (d, step): remote(
                slab_in.at[t, lane, chip_at(step)],
                slab_in.at[t, lane, chip_at(step)],
                relay_sem.at[t, d - 1, step],
                chip * rounds + lane_at(d),
            )
            for d in range(1, rounds)
            for step in range(chips)
        }
        for t in range(3)
    ]
    row_sums = []
    for step in range(1, devices):
        peer = lax.rem(me + step, devices)
        unit = lax.div(lax.div(peer, rounds), split) * rounds + lax.rem(peer, rounds)
        row_sums.append(remote(sums_out.at[unit], sums_in_rows.at[me], rows_sem.at[step - 1], peer))
    shares = [
        {
            (d, step): remote(
                part_out.at[d - 1, chip_at(step)],
                part_in.at[t, d - 1, chip_at(step)],
                part_sem.at[t, d - 1, step],
                chip * rounds + lane_at(d),
            )
            for d in range(1, rounds)
            for step in range(chips)
        }
        for t in range(2)
    ]
    homes = [
        {
            step: remote(
                home_out.at[t, chip_at(step)],
                home_in.at[t, chip],
                home_sem.at[t, step - 1],
                chip_at(step) * rounds + lane,
            )
            for step in range(1, chips)
        }
        for t in range(2)
    ]
    gains = []
    for step in range(1, devices):
        peer = lax.rem(me + step, devices)
        gains.append(remote(gain_out.at[peer], gain_back.at[me], gain_sem.at[step - 1], peer))

    bits = devices.bit_length() - 1
    first_slot = [devices - (devices >> k) for k in range(bits)]
    top = lax.div(chip, chips // 2)
    sections = 2
    by_section = [list(range(bits)), [0, *range(2, bits - 1), 1, bits - 1]]
    bit_orders = by_section * 2
    streams = len(bit_orders)
    half_width = width // 2
    piece = half_width // sections

    def half_start(group):
        return pl.multiple_of(half_width * (top + group - 2 * top * group), half_width)

    def physical(stream, mask):
        return sum(1 << bit_orders[stream][k] for k in range(bits) if mask >> k & 1)

    def sums_copy(half, stream, k, mask):
        slot = first_slot[k] + (mask >> (k + 1))
        if k == 0:
            source = weights.at[half, stream, flipped(me, physical(stream, mask))]
        else:
            source = sums_run.at[half, stream, mask >> 1]
        landing = stream if k < bits - 1 else (stream + sections) % streams
        return pltpu.make_async_remote_copy(
            src_ref=source,
            dst_ref=sums_in.at[half, landing, slot],
            send_sem=sums_sem.at[half, stream, slot, 0],
            recv_sem=sums_sem.at[half, landing, slot, 1],
            device_id={"tok": flipped(me, 1 << bit_orders[stream][k])},
            device_id_type=MESH,
        )

    stages = [
        [
            [
                {m: sums_copy(half, stream, k, m) for m in range(1 << k, devices, 2 << k)}
                for stream in range(streams)
            ]
            for half in range(2)
        ]
        for k in range(bits)
    ]
    far_first = sorted(range(1, chips), key=lambda step: (-step.bit_length(), step))
    near_first = list(range(1, chips))

    def send_slabs(t):
        for step in far_first:
            slabs[t][step].start()
        slab_in[t, lane, chip] = slab_out[t, lax.div(chip, split)]

    with jax.named_scope("first"):
        loads["sums"].wait()
        for hashing in range(rounds):
            for head in range(heads):
                sums_out[head * rounds + hashing] = sums_ref[hashing, head : head + 1, :]
        for load in cot_loads:
            load.wait()
        for name in ("tokens", "gain", "qk", "v", "order"):
            loads[name].start()
    with jax.named_scope("barrier"):
        pl.semaphore_wait(barrier, devices - 1)
    with jax.named_scope("sends"):
        for copy in row_sums:
            copy.start()
        send_slabs(0)
        own_unit = lax.div(chip, split) * rounds + lane
        sums_in_rows[me] = sums_out[own_unit]
        loads["tokens"].wait()
        loads["gain"].wait()
        normal[...] = normal_of(tokens_ref[...].astype(F32), gain_ref[...])
        loads["qk"].wait()
        query = dot_nn(normal[...], qk_ref[...]).astype(BF16)
        for head, part in enumerate(parts):
            slab_out[1, head] = query[:, part]
        send_slabs(1)
        loads["v"].wait()
        value = dot_nn(normal[...], v_ref[...]).astype(BF16)
        for head, part in enumerate(parts):
            slab_out[2, head] = value[:, part]
        send_slabs(2)
        for t in range(3):
            for d in range(1, rounds):
                relays[t][d, 0].start()
        loads["order"].wait()

    token_ids = lax.broadcasted_iota(jnp.int32, (rows, rows), 0)

    def tables(place):
        block = lax.rem(first + (place + base - 1 + blocks), blocks)
        start = pl.multiple_of(block * rows, rows)
        order = order_ref[pl.ds(lane, 1), pl.ds(start, rows)]
        chosen = one_hot_rows(slot_row(order, rows, stride), slot_count)
        pick[place] = chosen
        within = jnp.where(token_ids == lax.rem(order, jnp.int32(rows)), 1.0, 0.0).astype(BF16)
        moved = dot_nt(chosen, within).astype(BF16)
        spread[:, place] = moved.reshape(devices, stride, rows)

    with jax.named_scope("tables"):
        looped(held, 4, tables)

    def bucket_rows(t, source_chip, source_lane):
        source = source_chip * rounds + source_lane
        table = spread[source].reshape(held * stride, rows)
        placed = dot_nn(table, slab_in[t, source_lane, source_chip]).astype(BF16)
        bucket[source] = placed.reshape(held, stride, depth)

    def take_slabs(t):
        with jax.named_scope(f"take{t}"):
            for step in near_first:
                slabs[t][step].wait_recv()
                for d in range(1, rounds):
                    relays[t][d, step].start()

    def gather(t):
        with jax.named_scope(f"gather{t}"):
            looped(chips, 8, lambda place: bucket_rows(t, place, lane))
            for d in range(1, rounds):
                for step in [0, *near_first]:
                    relays[t][d, step].wait_recv()
                looped(chips, 8, lambda place: bucket_rows(t, place, lane_behind(d)))

    def sorted_rows(place):
        data = bucket[:, place].reshape(slot_count, depth)
        return dot_tn(pick[place], data).astype(BF16)

    def sort_queries(place):
        q = sorted_rows(place)
        sorted_q[place + base] = q
        sorted_k[place + base] = unit_of(q.astype(F32))

    def sort_cotangents(place):
        sorted_g[place + base] = sorted_rows(place)

    take_slabs(0)
    gather(0)
    with jax.named_scope("sortg"):
        looped(held, 16, sort_cotangents)
    take_slabs(1)
    gather(1)
    with jax.named_scope("sortq"):
        looped(held, 16, sort_queries)
    if split == 1:
        sorted_k[0] = sorted_k[queries]
    with jax.named_scope("rowsums"):
        for copy in row_sums:
            copy.wait_recv()
    diagonal = lax.broadcasted_iota(jnp.int32, (2 * rows, rows), 0) == rows + (
        lax.broadcasted_iota(jnp.int32, (2 * rows, rows), 1)
    )

    def probabilities(i):
        keys = sorted_k[pl.ds(i, 2)].reshape(2 * rows, depth)
        scores = dot_nt(keys, sorted_q[i + 1]) - sums_in_rows[first + i]
        probs[i + 1] = jnp.where(diagonal, 0.0, jnp.exp(scores)).astype(BF16)

    with jax.named_scope("probs"):
        looped(queries, 8, probabilities)
    if split > 1:
        probs[0] = jnp.zeros((2 * rows, rows), BF16)
        probs[queries + 1] = jnp.zeros((2 * rows, rows), BF16)
        sorted_g[queries + 1] = jnp.zeros((rows, depth), BF16)

    def after(j):
        return lax.rem(j, queries) + 1 if split == 1 else j + 1

    def bucket_back(place):
        placed = dot_nn(pick[place], sorted_v[place + base]).astype(BF16)
        bucket[:, place] = placed.reshape(devices, stride, depth)

    def home_rows(source_chip, source_lane):
        source = source_chip * rounds + source_lane
        table = spread[source].reshape(held * stride, rows)
        return dot_tn(table, bucket[source].reshape(held * stride, depth))

    def send_home(t):
        with jax.named_scope(f"home{t}"):
            if t > 0:
                for copy in shares[t - 1].values():
                    copy.wait_send()
            for d in range(1, rounds):

                def share(place):
                    part_out[d - 1, place] = home_rows(place, lane_at(d)).astype(BF16)

                looped(chips, 8, share)
                for step in [*far_first, 0]:
                    shares[t][d, step].start()

            def keep(place):
                d_query[place] = home_rows(place, lane)

            looped(chips, 8, keep)
            for step in [*far_first, 0]:
                for d in range(1, rounds):
                    shares[t][d, step].wait_recv()
            for place in range(chips):
                total = d_query[place]
                for d in range(1, rounds):
                    total += part_in[t, d - 1, place].astype(F32)
                home_out[t, place] = total.astype(BF16)
            for step in far_first:
                homes[t][step].start()
            home_in[t, chip] = home_out[t, chip]

    def value_gradients(place):
        j = place + base
        grad = dot_nn(probs[j, rows:, :], sorted_g[j])
        grad += dot_nn(probs[after(j), :rows, :], sorted_g[after(j)])
        sorted_v[j] = grad.astype(BF16)

    with jax.named_scope("dv"):
        looped(held, 16, value_gradients)
        looped(held, 16, bucket_back)
    send_home(0)
    take_slabs(2)
    gather(2)

    def sort_values(place):
        sorted_v[place + base] = sorted_rows(place)

    with jax.named_scope("sortv"):
        looped(held, 16, sort_values)
    if split == 1:
        sorted_v[0] = sorted_v[queries]
    else:
        d_query[0] = jnp.zeros((rows, depth), F32)
        sorted_q[queries + 1] = jnp.zeros((rows, depth), BF16)

    def score_gradients(i):
        j = i + 1
        values = sorted_v[pl.ds(i, 2)].reshape(2 * rows, depth)
        w = probs[j].astype(F32)
        d_probs = dot_nt(values, sorted_g[j])
        delta = jnp.sum(w * d_probs, axis=0, keepdims=True)
        probs[j] = (w * (d_probs - delta)).astype(BF16)

    def query_gradients(i):
        keys = sorted_k[pl.ds(i, 2)].reshape(2 * rows, depth)
        d_query[i + 1] = dot_tn(probs[i + 1], keys)

    def key_gradients(place):
        j = place + base
        q = sorted_q[j].astype(F32)
        dk = dot_nn(probs[j, rows:, :], sorted_q[j])
        dk += dot_nn(probs[after(j), :rows, :], sorted_q[after(j)])
        scale = lax.rsqrt(jnp.mean(q * q, axis=-1, keepdims=True) + EPS)
        along = jnp.mean(q * dk, axis=-1, keepdims=True)
        pulled = (dk * scale - q * (scale * scale * scale * along)) / math.sqrt(depth)
        sorted_v[j] = (d_query[j] + pulled).astype(BF16)

    def assemble(t, group):
        steps = [m for m in near_first if m.bit_length() <= bits - 2]
        if group == 1:
            steps = [m for m in near_first if m.bit_length() > bits - 2]
        with jax.named_scope(f"wait_home{t}_{group}"):
            for step in steps:
                homes[t][step].wait_recv()
        half_heads = heads // 2
        start = half_heads * (top + group - 2 * top * group)
        for place in range(half_heads):
            total = home_in[t, (start + place) * split]
            for p in range(1, split):
                other = home_in[t, (start + place) * split + p]
                total = (total.astype(F32) + other.astype(F32)).astype(BF16)
            grads[t, group, :, parts[place]] = total

    def weight_gradient(t, half, group):
        with jax.named_scope(f"weight{half}_{group}"):
            mine = range(group * sections, (group + 1) * sections)
            for section, stream in enumerate(mine):
                columns = slice(section * piece, (section + 1) * piece)
                grad = dot_tn(normal[...], grads[t, group, :, columns]) * grad_scale
                weights[half, stream] = grad.astype(BF16).reshape(devices, share, piece)
            for stream in mine:
                for mask in forwarding_order(stages[0][half][stream]):
                    stages[0][half][stream][mask].start()

    def row_gradient(t, group, weight_ref):
        return dot_nt(grads[t, group], weight_ref[:, pl.ds(half_start(group), half_width)])

    outs = (d_qk_ref, d_v_ref)

    def run_sums(half, k, group):
        mine = range(group * sections, (group + 1) * sections)
        waiting = []
        with jax.named_scope(f"sum{half}_{k}_{group}"):
            for masks in zip(*[forwarding_order(stages[k][half][s]) for s in mine]):
                for stream, mask in zip(mine, masks):
                    rest = mask - (1 << k)
                    sender = stream if k < bits - 1 else (stream + sections) % streams
                    stages[k][half][sender][mask].wait_recv()
                    slot = first_slot[k] + (mask >> (k + 1))
                    came = sums_in[half, stream, slot].astype(F32)
                    if k == 0:
                        before = weights[half, stream, flipped(me, physical(stream, rest))]
                    else:
                        before = sums_run[half, stream, rest >> 1]
                    run = before.astype(F32) + came
                    if k == bits - 1:
                        column = half_start(group) + (stream - mine[0]) * piece
                        outs[half][:, pl.ds(pl.multiple_of(column, piece), piece)] = run
                        continue
                    sums_run[half, stream, rest >> 1] = run.astype(BF16)
                    waiting.append(stages[k + 1][half][stream].get(rest))
                    if len(waiting) > 1:
                        onward = waiting.pop(0)
                        if onward is not None:
                            onward.start()
            for onward in waiting:
                if onward is not None:
                    onward.start()

    share = width // devices
    with jax.named_scope("ds"):
        looped(queries, 16, score_gradients)
    with jax.named_scope("dq"):
        looped(queries, 16, query_gradients)
    with jax.named_scope("dk"):
        looped(held, 16, key_gradients)
    with jax.named_scope("back"):
        looped(held, 16, bucket_back)
    send_home(1)
    assemble(0, 0)
    weight_gradient(0, 1, 0)
    assemble(0, 1)
    weight_gradient(0, 1, 1)
    run_sums(1, 0, 0)
    run_sums(1, 0, 1)
    d_normal = row_gradient(0, 0, v_ref) + row_gradient(0, 1, v_ref)
    assemble(1, 0)
    weight_gradient(1, 0, 0)
    d_normal += row_gradient(1, 0, qk_ref)
    run_sums(0, 0, 0)
    run_sums(1, 1, 0)
    run_sums(1, 1, 1)
    assemble(1, 1)
    weight_gradient(1, 0, 1)
    d_normal += row_gradient(1, 1, qk_ref)
    run_sums(0, 0, 1)
    with jax.named_scope("rows"):
        x = tokens_ref[...].astype(F32)
        scale = lax.rsqrt(jnp.mean(x * x, axis=-1, keepdims=True) + EPS)
        gain_total = jnp.sum(d_normal * (x * scale), axis=0, keepdims=True) * grad_scale
        share = width // devices
        gain_out[...] = jnp.zeros(gain_out.shape, F32)
        for device in range(devices):
            gain_out[device, 0:1, 0:share] = gain_total[:, device * share : (device + 1) * share]
        gain_back[me] = gain_out[me]
        for copy in gains:
            copy.start()
        t = d_normal * gain_ref[...]
        along = jnp.mean(x * t, axis=-1, keepdims=True)
        d_tokens_ref[...] = (t * scale - x * (scale * scale * scale * along)).astype(BF16)

    run_sums(0, 1, 0)
    run_sums(1, 2, 0)
    run_sums(1, 2, 1)
    run_sums(0, 1, 1)
    for k in range(2, bits):
        run_sums(0, k, 0)
        if k > 2:
            run_sums(1, k, 0)
            run_sums(1, k, 1)
        run_sums(0, k, 1)
    with jax.named_scope("sendwaits"):
        for copy in gains:
            copy.wait_recv()
        d_gain_ref[...] = jnp.sum(gain_back[:, 0, :], axis=0, keepdims=True)
        for stage in stages:
            for half in stage:
                for stream in half:
                    for copy in stream.values():
                        copy.wait_send()
        for group in [*slabs, *relays, shares[-1], *homes]:
            for copy in group.values():
                copy.wait_send()
        for copy in [*row_sums, *gains]:
            copy.wait_send()


def hand_over(share, d_tokens_in, d_gain_in, d_qk_in, d_v_in, d_tokens, d_gain, d_qk, d_v):
    d_tokens[...] = d_tokens_in[...]
    d_gain[...] = d_gain_in[:, :share]
    d_qk[...] = d_qk_in[...]
    d_v[...] = d_v_in[...]


def per_device(tokens, norm_gain, w_qk, w_v, cotangent, log_sums, bucket_order, token_position):
    devices = lax.axis_size("tok")
    tok_dev, width = tokens.shape
    rounds, seq_len = bucket_order.shape
    heads = log_sums.shape[1]
    units = rounds * heads
    assert tok_dev == BLOCK and devices % units == 0
    split = devices // units
    chips = devices // rounds
    depth = width // heads
    queries = seq_len // tok_dev // split
    held = queries if split == 1 else queries + 1
    capacity = 5 * tok_dev // (4 * devices)
    stride = -(-capacity // 8) * 8
    grad_scale = 1.0 / math.sqrt(seq_len)
    share = width // devices
    dma = pltpu.SemaphoreType.DMA

    def low(*shape):
        return pltpu.VMEM(shape, BF16)

    def full(*shape):
        return pltpu.VMEM(shape, F32)

    results = pl.pallas_call(
        functools.partial(core_kernel, heads, stride, split, grad_scale),
        out_shape=[
            jax.ShapeDtypeStruct((tok_dev, width), BF16),
            jax.ShapeDtypeStruct((1, 128), F32),
            jax.ShapeDtypeStruct((share, width), F32),
            jax.ShapeDtypeStruct((share, width), F32),
        ],
        in_specs=[pl.BlockSpec(memory_space=pl.ANY)] * 7,
        out_specs=whole(4),
        scratch_shapes=[
            full(1, width),
            pltpu.VMEM((rounds, seq_len), jnp.int32),
            full(rounds, heads, tok_dev),
            low(tok_dev, width),
            low(width, width),
            low(width, width),
            low(tok_dev, width),
            low(3, heads, tok_dev, depth),
            low(3, rounds, chips, tok_dev, depth),
            full(units, 1, tok_dev),
            full(devices, 1, tok_dev),
            low(devices, held, stride, tok_dev),
            low(held, devices * stride, tok_dev),
            low(devices, held, stride, depth),
            *[low(queries + 2, tok_dev, depth)] * 4,
            low(queries + 2, 2 * tok_dev, tok_dev),
            full(queries + 2, tok_dev, depth),
            low(rounds - 1, chips, tok_dev, depth),
            low(2, rounds - 1, chips, tok_dev, depth),
            *[low(2, chips, tok_dev, depth)] * 2,
            low(2, 2, tok_dev, width // 2),
            *[full(devices, 8, 128)] * 2,
            low(2, 4, devices, share, width // 4),
            low(2, 4, devices - 1, share, width // 4),
            low(2, 4, devices // 2, share, width // 4),
            dma((heads,)),
            dma((6,)),
            dma((3, chips - 1, 2)),
            dma((3, rounds - 1, chips, 2)),
            dma((devices - 1, 2)),
            dma((2, rounds - 1, chips, 2)),
            dma((2, chips - 1, 2)),
            dma((devices - 1, 2)),
            dma((2, 4, devices - 1, 2)),
        ],
        compiler_params=pltpu.CompilerParams(
            vmem_limit_bytes=VMEM_LIMIT, collective_id=0, has_side_effects=True
        ),
        name="core",
    )(norm_gain.reshape(1, width), bucket_order, log_sums, tokens, cotangent, w_qk, w_v)
    d_tokens, d_gain, d_qk, d_v = pl.pallas_call(
        functools.partial(hand_over, share),
        out_shape=[
            jax.ShapeDtypeStruct((tok_dev, width), BF16),
            jax.ShapeDtypeStruct((1, share), F32),
            jax.ShapeDtypeStruct((share, width), F32),
            jax.ShapeDtypeStruct((share, width), F32),
        ],
        in_specs=whole(4),
        out_specs=whole(4),
        name="hand_over",
    )(*results)
    return (d_tokens, d_gain.reshape(share), d_qk, d_v)


def solution(mesh):
    in_specs = (
        P(("groups", "tok"), None),
        P(),
        P(),
        P(),
        P(("groups", "tok"), None),
        P(None, None, ("groups", "tok")),
        P(None, "groups"),
        P(None, ("groups", "tok")),
    )
    out_specs = (
        P(("groups", "tok"), None),
        P(("groups", "tok")),
        P(("groups", "tok"), None),
        P(("groups", "tok"), None),
    )
    return jax.shard_map(
        per_device, mesh=mesh, in_specs=in_specs, out_specs=out_specs, check_vma=False
    )
```

```python
import functools
import math

import jax
import jax.numpy as jnp
from jax import lax
from jax.experimental import pallas as pl
from jax.experimental.pallas import tpu as pltpu
from jax.sharding import PartitionSpec as P

BLOCK = 256
EPS = 1e-06
VMEM_LIMIT = 62 * 1024 * 1024
MESH = pl.DeviceIdType.MESH
F32 = jnp.float32
BF16 = jnp.bfloat16


def whole(count):
    return [pl.BlockSpec(memory_space=pltpu.VMEM)] * count


def dot_nn(a, b):
    return lax.dot_general(a, b, (((1,), (0,)), ((), ())), preferred_element_type=F32)


def dot_nt(a, b):
    return lax.dot_general(a, b, (((1,), (1,)), ((), ())), preferred_element_type=F32)


def dot_tn(a, b):
    return lax.dot_general(a, b, (((0,), (0,)), ((), ())), preferred_element_type=F32)


def slot_row(order, tok_dev, stride):
    size = order.shape[1]
    owner = lax.div(order, jnp.int32(tok_dev))
    owner_col = jnp.broadcast_to(owner, (size, size)).T
    before = lax.broadcasted_iota(jnp.int32, (size, size), 0) < lax.broadcasted_iota(
        jnp.int32, (size, size), 1
    )
    earlier = (owner_col == owner) & before
    rank = jnp.sum(earlier.astype(F32), axis=0, keepdims=True).astype(jnp.int32)
    return owner * stride + rank


def one_hot_rows(slots, slot_count):
    size = slots.shape[1]
    ids = lax.broadcasted_iota(jnp.int32, (slot_count, size), 0)
    return jnp.where(ids == slots, 1.0, 0.0).astype(BF16)


def normal_of(x, gain):
    return (x * lax.rsqrt(jnp.mean(x * x, axis=-1, keepdims=True) + EPS) * gain).astype(BF16)


def unit_of(q):
    depth = q.shape[-1]
    scale = lax.rsqrt(jnp.mean(q * q, axis=-1, keepdims=True) + EPS)
    return (q * scale / math.sqrt(depth)).astype(BF16)


def flipped(index, mask):
    bit = 1
    while bit <= mask:
        if mask & bit:
            index = index + bit * (1 - 2 * lax.rem(lax.div(index, bit), 2))
        bit *= 2
    return index


def forwarding_order(masks):
    return sorted(masks, key=lambda m: int(bin(m)[:1:-1].ljust(16, "0"), 2), reverse=True)


def looped(count, unroll, body):
    steps = count // unroll

    def step(i, carry):
        for u in range(unroll):
            body(i * unroll + u)
        return carry

    if steps > 1:
        lax.fori_loop(0, steps, step, 0)
    for i in range(steps * unroll if steps > 1 else 0, count):
        body(i)


def core_kernel(heads, stride, split, grad_scale, *refs):
    gain_hbm, order_hbm, sums_hbm, tokens_hbm, cot_hbm, qk_hbm, v_hbm = refs[:7]
    d_tokens_ref, d_gain_ref, d_weights_ref = refs[7:10]
    (
        gain_ref, order_ref, sums_ref, tokens_ref, maps,
        normal, slab_out, slab_in, sums_out, sums_in_rows, spread, pick, bucket,
        sorted_q, sorted_k, sorted_g, sorted_v, probs, d_query,
        part_out, part_in, home_out, home_in, grads, rows_kept, rows_out, rows_in, ends, ends_in,
        gain_out, gain_back, weights, sums_in, sums_run,
        cot_sem, load_sem, slab_sem, relay_sem, rows_sem, part_sem, home_send_sem,
        home_recv_sem, gain_sem, sums_sem, pair_sem,
    ) = refs[10:]
    devices = lax.axis_size("tok")
    me = lax.axis_index("tok")
    rounds, seq_len = order_ref.shape
    rows, width = tokens_ref.shape
    depth = width // heads
    chips = devices // rounds
    chip, lane = lax.div(me, rounds), lax.rem(me, rounds)
    blocks = seq_len // rows
    queries = blocks // split
    first = lax.rem(chip, split) * queries
    base = 1 if split == 1 else 0
    held = queries + 1 - base
    slot_count = devices * stride
    parts = [slice(head * depth, (head + 1) * depth) for head in range(heads)]

    def remote(src, dst, sems, peer):
        return pltpu.make_async_remote_copy(
            src_ref=src,
            dst_ref=dst,
            send_sem=sems.at[0],
            recv_sem=sems.at[1],
            device_id={"tok": peer},
            device_id_type=MESH,
        )

    barrier = pltpu.get_barrier_semaphore()
    for step in range(1, devices):
        peer = lax.rem(me + step, devices)
        pl.semaphore_signal(barrier, inc=1, device_id={"tok": peer}, device_id_type=MESH)
    cot_loads = [
        pltpu.make_async_copy(cot_hbm.at[:, part], slab_out.at[0, head], cot_sem.at[head])
        for head, part in enumerate(parts)
    ]
    loads = {
        name: pltpu.make_async_copy(src, dst, load_sem.at[place])
        for place, (name, src, dst) in enumerate(
            [
                ("sums", sums_hbm, sums_ref),
                ("tokens", tokens_hbm, tokens_ref),
                ("gain", gain_hbm, gain_ref),
                ("qk", qk_hbm, maps.at[1]),
                ("v", v_hbm, maps.at[0]),
                ("order", order_hbm, order_ref),
            ]
        )
    }
    loads["sums"].start()
    for load in cot_loads:
        load.start()

    def chip_at(step):
        return flipped(chip, step)

    def lane_at(step):
        return lax.rem(lane + step, rounds)

    def lane_behind(step):
        return lax.rem(lane + rounds - step, rounds)

    slabs = [
        {
            step: remote(
                slab_out.at[t, lax.div(chip_at(step), split)],
                slab_in.at[t, lane, chip],
                slab_sem.at[t, step - 1],
                chip_at(step) * rounds + lane,
            )
            for step in range(1, chips)
        }
        for t in range(3)
    ]
    relays = [
        {
            (d, step): remote(
                slab_in.at[t, lane, chip_at(step)],
                slab_in.at[t, lane, chip_at(step)],
                relay_sem.at[t, d - 1, step],
                chip * rounds + lane_at(d),
            )
            for d in range(1, rounds)
            for step in range(chips)
        }
        for t in range(3)
    ]
    row_sums = []
    for step in range(1, devices):
        peer = lax.rem(me + step, devices)
        unit = lax.div(lax.div(peer, rounds), split) * rounds + lax.rem(peer, rounds)
        row_sums.append(remote(sums_out.at[unit], sums_in_rows.at[me], rows_sem.at[step - 1], peer))
    shares = [
        {
            (d, step): remote(
                part_out.at[d - 1, chip_at(step)],
                part_in.at[t, d - 1, chip_at(step)],
                part_sem.at[t, d - 1, step],
                chip * rounds + lane_at(d),
            )
            for d in range(1, rounds)
            for step in range(chips)
        }
        for t in range(2)
    ]
    homes = [
        [
            pltpu.make_async_remote_copy(
                src_ref=home_out.at[t, chip_at(step)],
                dst_ref=home_in.at[lane, chip],
                send_sem=home_send_sem.at[t, step],
                recv_sem=home_recv_sem.at[step, lane],
                device_id={"tok": chip_at(step) * rounds + t},
                device_id_type=MESH,
            )
            for step in range(chips)
        ]
        for t in range(2)
    ]
    comings = [
        [
            pltpu.make_async_remote_copy(
                src_ref=home_out.at[0, chip_at(step)],
                dst_ref=home_in.at[l, chip_at(step)],
                send_sem=home_send_sem.at[0, step],
                recv_sem=home_recv_sem.at[step, l],
                device_id={"tok": chip * rounds + 1 - lane},
                device_id_type=MESH,
            )
            for l in range(rounds)
        ]
        for step in range(chips)
    ]
    other = 1 - lane
    sibling = chip * rounds + other
    normal_copy = remote(normal.at[lane], normal.at[lane], pair_sem.at[0], sibling)
    rows_copy = remote(rows_out, rows_in, pair_sem.at[1], sibling)
    gains = []
    for step in range(1, devices):
        peer = lax.rem(me + step, devices)
        gains.append(remote(gain_out.at[peer], gain_back.at[me], gain_sem.at[step - 1], peer))

    bits = chips.bit_length() - 1
    first_slot = [chips - (chips >> k) for k in range(bits)]
    top = lax.div(chip, chips // 2)
    half_width = width // 2
    y_first, y_late = list(range(bits)), [*range(1, bits - 1), 0, bits - 1]
    late_start = 3 * half_width // 4
    sections = [(y_first, slice(0, late_start)), (y_late, slice(late_start, half_width))]

    def half_start(group):
        return pl.multiple_of(half_width * (top + group - 2 * top * group), half_width)

    def physical(bit_order, mask):
        return sum(1 << bit_order[k] for k in range(bits) if mask >> k & 1)

    def sums_copy(group, place, k, mask):
        bit_order, columns = sections[place]
        slot = first_slot[k] + (mask >> (k + 1))
        if k == 0:
            source = weights.at[group, flipped(chip, physical(bit_order, mask)), :, columns]
        else:
            source = sums_run.at[group, mask >> 1, :, columns]
        landing = group if k < bits - 1 else 1 - group
        return pltpu.make_async_remote_copy(
            src_ref=source,
            dst_ref=sums_in.at[landing, slot, :, columns],
            send_sem=sums_sem.at[group, place, slot, 0],
            recv_sem=sums_sem.at[landing, place, slot, 1],
            device_id={"tok": flipped(chip, 1 << bit_order[k]) * rounds + lane},
            device_id_type=MESH,
        )

    stages = [
        [
            [
                {m: sums_copy(group, p, k, m) for m in range(1 << k, chips, 2 << k)}
                for p in range(len(sections))
            ]
            for group in range(2)
        ]
        for k in range(bits)
    ]
    end_copies = [
        remote(
            ends.at[other, :, pl.ds(half_start(group), half_width)],
            ends_in.at[:, pl.ds(half_start(group), half_width)],
            pair_sem.at[2 + group],
            sibling,
        )
        for group in range(2)
    ]
    far_first = sorted(range(1, chips), key=lambda step: (-step.bit_length(), step))
    near_first = list(range(1, chips))

    def send_slabs(t):
        for step in far_first:
            slabs[t][step].start()
        slab_in[t, lane, chip] = slab_out[t, lax.div(chip, split)]

    with jax.named_scope("first"):
        loads["sums"].wait()
        for hashing in range(rounds):
            for head in range(heads):
                sums_out[head * rounds + hashing] = sums_ref[hashing, head : head + 1, :]
        for load in cot_loads:
            load.wait()
        for name in ("tokens", "gain", "qk", "v", "order"):
            loads[name].start()
    with jax.named_scope("barrier"):
        pl.semaphore_wait(barrier, devices - 1)
    with jax.named_scope("sends"):
        for copy in row_sums:
            copy.start()
        send_slabs(0)
        own_unit = lax.div(chip, split) * rounds + lane
        sums_in_rows[me] = sums_out[own_unit]
        loads["tokens"].wait()
        loads["gain"].wait()
        rows_now = normal_of(tokens_ref[...].astype(F32), gain_ref[...])
        normal[lane] = rows_now
        loads["qk"].wait()
        query = dot_nn(rows_now, maps[1]).astype(BF16)
        for head, part in enumerate(parts):
            slab_out[1, head] = query[:, part]
        send_slabs(1)
        loads["v"].wait()
        value = dot_nn(normal[lane], maps[0]).astype(BF16)
        for head, part in enumerate(parts):
            slab_out[2, head] = value[:, part]
        send_slabs(2)
        normal_copy.start()
        for t in range(3):
            for d in range(1, rounds):
                relays[t][d, 0].start()
        loads["order"].wait()

    token_ids = lax.broadcasted_iota(jnp.int32, (rows, rows), 0)

    def tables(place):
        block = lax.rem(first + (place + base - 1 + blocks), blocks)
        start = pl.multiple_of(block * rows, rows)
        order = order_ref[pl.ds(lane, 1), pl.ds(start, rows)]
        chosen = one_hot_rows(slot_row(order, rows, stride), slot_count)
        pick[place] = chosen
        within = jnp.where(token_ids == lax.rem(order, jnp.int32(rows)), 1.0, 0.0).astype(BF16)
        moved = dot_nt(chosen, within).astype(BF16)
        spread[:, place] = moved.reshape(devices, stride, rows)

    with jax.named_scope("tables"):
        looped(held, 4, tables)

    def bucket_rows(t, source_chip, source_lane):
        source = source_chip * rounds + source_lane
        table = spread[source].reshape(held * stride, rows)
        placed = dot_nn(table, slab_in[t, source_lane, source_chip]).astype(BF16)
        bucket[source] = placed.reshape(held, stride, depth)

    def take_slabs(t):
        with jax.named_scope(f"take{t}"):
            for step in near_first:
                slabs[t][step].wait_recv()
                for d in range(1, rounds):
                    relays[t][d, step].start()

    def gather(t):
        with jax.named_scope(f"gather{t}"):
            looped(chips, 8, lambda place: bucket_rows(t, place, lane))
            for d in range(1, rounds):
                for step in [0, *near_first]:
                    relays[t][d, step].wait_recv()
                looped(chips, 8, lambda place: bucket_rows(t, place, lane_behind(d)))

    def sorted_rows(place):
        data = bucket[:, place].reshape(slot_count, depth)
        return dot_tn(pick[place], data).astype(BF16)

    def sort_queries(place):
        q = sorted_rows(place)
        sorted_q[place + base] = q
        sorted_k[place + base] = unit_of(q.astype(F32))

    def sort_cotangents(place):
        sorted_g[place + base] = sorted_rows(place)

    take_slabs(0)
    gather(0)
    with jax.named_scope("sortg"):
        looped(held, 16, sort_cotangents)
    take_slabs(1)
    gather(1)
    with jax.named_scope("sortq"):
        looped(held, 16, sort_queries)
    if split == 1:
        sorted_k[0] = sorted_k[queries]
    with jax.named_scope("rowsums"):
        for copy in row_sums:
            copy.wait_recv()
    diagonal = lax.broadcasted_iota(jnp.int32, (2 * rows, rows), 0) == rows + (
        lax.broadcasted_iota(jnp.int32, (2 * rows, rows), 1)
    )

    def probabilities(i):
        keys = sorted_k[pl.ds(i, 2)].reshape(2 * rows, depth)
        scores = dot_nt(keys, sorted_q[i + 1]) - sums_in_rows[first + i]
        probs[i + 1] = jnp.where(diagonal, 0.0, jnp.exp(scores)).astype(BF16)

    with jax.named_scope("probs"):
        looped(queries, 8, probabilities)
    if split > 1:
        probs[0] = jnp.zeros((2 * rows, rows), BF16)
        probs[queries + 1] = jnp.zeros((2 * rows, rows), BF16)
        sorted_g[queries + 1] = jnp.zeros((rows, depth), BF16)

    def after(j):
        return lax.rem(j, queries) + 1 if split == 1 else j + 1

    def bucket_back(place):
        placed = dot_nn(pick[place], sorted_v[place + base]).astype(BF16)
        bucket[:, place] = placed.reshape(devices, stride, depth)

    def home_rows(source_chip, source_lane):
        source = source_chip * rounds + source_lane
        table = spread[source].reshape(held * stride, rows)
        return dot_tn(table, bucket[source].reshape(held * stride, depth))

    def send_home(t):
        with jax.named_scope(f"home{t}"):
            if t > 0:
                for copy in shares[t - 1].values():
                    copy.wait_send()
            for d in range(1, rounds):

                def share(place):
                    part_out[d - 1, place] = home_rows(place, lane_at(d)).astype(BF16)

                looped(chips, 8, share)
                for step in [*far_first, 0]:
                    shares[t][d, step].start()

            def keep(place):
                d_query[place] = home_rows(place, lane)

            looped(chips, 8, keep)
            if t == 0:
                take_slabs(2)
            for step in [*far_first, 0]:
                for d in range(1, rounds):
                    shares[t][d, step].wait_recv()
            for place in range(chips):
                total = d_query[place]
                for d in range(1, rounds):
                    total += part_in[t, d - 1, place].astype(F32)
                home_out[t, place] = total.astype(BF16)
            for step in near_first:
                homes[t][step].start()

            @pl.when(lane == t)
            def _():
                home_in[lane, chip] = home_out[t, chip]

            @pl.when(lane != t)
            def _():
                homes[t][0].start()


    def value_gradients(place):
        j = place + base
        grad = dot_nn(probs[j, rows:, :], sorted_g[j])
        grad += dot_nn(probs[after(j), :rows, :], sorted_g[after(j)])
        sorted_v[j] = grad.astype(BF16)

    with jax.named_scope("dv"):
        looped(held, 16, value_gradients)
        looped(held, 16, bucket_back)
    send_home(0)
    gather(2)

    def sort_values(place):
        sorted_v[place + base] = sorted_rows(place)

    with jax.named_scope("sortv"):
        looped(held, 16, sort_values)
    if split == 1:
        sorted_v[0] = sorted_v[queries]
    else:
        d_query[0] = jnp.zeros((rows, depth), F32)
        sorted_q[queries + 1] = jnp.zeros((rows, depth), BF16)

    def score_gradients(i):
        j = i + 1
        values = sorted_v[pl.ds(i, 2)].reshape(2 * rows, depth)
        w = probs[j].astype(F32)
        d_probs = dot_nt(values, sorted_g[j])
        delta = jnp.sum(w * d_probs, axis=0, keepdims=True)
        probs[j] = (w * (d_probs - delta)).astype(BF16)

    def query_gradients(i):
        keys = sorted_k[pl.ds(i, 2)].reshape(2 * rows, depth)
        d_query[i + 1] = dot_tn(probs[i + 1], keys)

    def key_gradients(place):
        j = place + base
        q = sorted_q[j].astype(F32)
        dk = dot_nn(probs[j, rows:, :], sorted_q[j])
        dk += dot_nn(probs[after(j), :rows, :], sorted_q[after(j)])
        scale = lax.rsqrt(jnp.mean(q * q, axis=-1, keepdims=True) + EPS)
        along = jnp.mean(q * dk, axis=-1, keepdims=True)
        pulled = (dk * scale - q * (scale * scale * scale * along)) / math.sqrt(depth)
        sorted_v[j] = (d_query[j] + pulled).astype(BF16)

    def assemble(group):
        steps = [m for m in range(chips) if (m.bit_length() == bits) == (group == 1)]
        with jax.named_scope(f"wait_home{group}"):
            for step in steps:
                if step > 0:
                    for coming in comings[step]:
                        coming.wait_recv()
                else:
                    pltpu.make_async_remote_copy(
                        src_ref=home_out.at[0, chip],
                        dst_ref=home_in.at[other, chip],
                        send_sem=home_send_sem.at[0, 0],
                        recv_sem=home_recv_sem.at[0, other],
                        device_id={"tok": sibling},
                        device_id_type=MESH,
                    ).wait_recv()
        half_heads = heads // 2
        start = half_heads * (top + group - 2 * top * group)
        for l in range(rounds):
            for place in range(half_heads):
                total = home_in[l, (start + place) * split]
                for p in range(1, split):
                    more = home_in[l, (start + place) * split + p]
                    total = (total.astype(F32) + more.astype(F32)).astype(BF16)
                grads[group, l * rows : (l + 1) * rows, parts[place]] = total

    def weight_gradient(group):
        with jax.named_scope(f"weight{group}"):
            normals = normal[...].reshape(rounds * rows, width)
            grad = dot_tn(normals, grads[group]) * grad_scale
            weights[group] = grad.astype(BF16).reshape(chips, width // chips, half_width)
            for copies in stages[0][group]:
                for mask in forwarding_order(copies):
                    copies[mask].start()

    def row_gradients(group):
        with jax.named_scope(f"rowgrad{group}"):
            columns = pl.ds(half_start(group), half_width)
            for l in range(rounds):
                part = dot_nt(grads[group, l * rows : (l + 1) * rows], maps[lane, :, columns])
                if group == 0:
                    rows_kept[l] = part
                else:
                    rows_kept[l] += part

    def run_sums(k, group):
        waiting = []
        with jax.named_scope(f"sum{k}_{group}"):
            for mask in forwarding_order(stages[k][group][0]):
                for place, (bit_order, columns) in enumerate(sections):
                    rest = mask - (1 << k)
                    sender = group if k < bits - 1 else 1 - group
                    stages[k][sender][place][mask].wait_recv()
                    slot = first_slot[k] + (mask >> (k + 1))
                    came = sums_in[group, slot, :, columns].astype(F32)
                    if k == 0:
                        row = flipped(chip, physical(bit_order, rest))
                        before = weights[group, row, :, columns]
                    else:
                        before = sums_run[group, rest >> 1, :, columns]
                    run = before.astype(F32) + came
                    if k == bits - 1:
                        column = pl.multiple_of(half_start(group) + columns.start, 128)
                        into = pl.ds(column, columns.stop - columns.start)
                        for l in range(rounds):
                            ends[l, :, into] = run[l * share : (l + 1) * share]
                        continue
                    sums_run[group, rest >> 1, :, columns] = run.astype(BF16)
                    waiting.append(stages[k + 1][group][place].get(rest))
                    if len(waiting) > 1:
                        onward = waiting.pop(0)
                        if onward is not None:
                            onward.start()
            for onward in waiting:
                if onward is not None:
                    onward.start()
            if k == bits - 1:
                end_copies[group].start()

    share = width // devices
    with jax.named_scope("ds"):
        looped(queries, 16, score_gradients)
    with jax.named_scope("dq"):
        looped(queries, 16, query_gradients)
    with jax.named_scope("dk"):
        looped(held, 16, key_gradients)
    with jax.named_scope("back"):
        looped(held, 16, bucket_back)
    send_home(1)
    normal_copy.wait_recv()
    assemble(0)
    weight_gradient(0)
    row_gradients(0)
    run_sums(0, 0)
    assemble(1)
    weight_gradient(1)
    row_gradients(1)
    rows_out[...] = rows_kept[other].astype(BF16)
    rows_copy.start()
    for k in range(1, bits - 1):
        run_sums(k, 0)
        run_sums(k - 1, 1)
    rows_copy.wait_recv()
    d_normal = rows_kept[lane] + rows_in[...].astype(F32)
    with jax.named_scope("rows"):
        x = tokens_ref[...].astype(F32)
        scale = lax.rsqrt(jnp.mean(x * x, axis=-1, keepdims=True) + EPS)
        gain_total = jnp.sum(d_normal * (x * scale), axis=0, keepdims=True) * grad_scale
        share = width // devices
        gain_out[...] = jnp.zeros(gain_out.shape, F32)
        for device in range(devices):
            gain_out[device, 0:1, 0:share] = gain_total[:, device * share : (device + 1) * share]
        gain_back[me] = gain_out[me]
        for copy in gains:
            copy.start()
        t = d_normal * gain_ref[...]
        along = jnp.mean(x * t, axis=-1, keepdims=True)
        d_tokens_ref[...] = (t * scale - x * (scale * scale * scale * along)).astype(BF16)

    run_sums(bits - 2, 1)
    run_sums(bits - 1, 0)
    run_sums(bits - 1, 1)
    with jax.named_scope("ends"):
        d_weights_ref[lane] = ends[lane]
        for copy in end_copies:
            copy.wait_recv()
        d_weights_ref[other] = ends_in[...]
    with jax.named_scope("sendwaits"):
        for copy in gains:
            copy.wait_recv()
        d_gain_ref[...] = jnp.sum(gain_back[:, 0, :], axis=0, keepdims=True)
        for stage in stages:
            for copies in [*stage[0], *stage[1]]:
                for copy in copies.values():
                    copy.wait_send()
        for group in [*slabs, *relays, shares[-1]]:
            for copy in group.values():
                copy.wait_send()
        for t in range(2):
            for step in range(1, chips):
                homes[t][step].wait_send()
        pltpu.make_async_remote_copy(
            src_ref=home_out.at[0, chip],
            dst_ref=home_in.at[lane, chip],
            send_sem=home_send_sem.at[other, 0],
            recv_sem=home_recv_sem.at[0, lane],
            device_id={"tok": sibling},
            device_id_type=MESH,
        ).wait_send()
        for copy in [*row_sums, *gains, normal_copy, rows_copy, *end_copies]:
            copy.wait_send()


def hand_over(share, d_tokens_in, d_gain_in, d_weights_in, d_tokens, d_gain, d_qk, d_v, sems):
    pairs = [
        (d_tokens_in, d_tokens), (d_weights_in.at[1], d_qk), (d_weights_in.at[0], d_v)
    ]
    copies = [pltpu.make_async_copy(*pair, sems.at[i]) for i, pair in enumerate(pairs)]
    for copy in copies:
        copy.start()
    d_gain[...] = d_gain_in[:, :share]
    for copy in copies:
        copy.wait()


def per_device(tokens, norm_gain, w_qk, w_v, cotangent, log_sums, bucket_order, token_position):
    devices = lax.axis_size("tok")
    tok_dev, width = tokens.shape
    rounds, seq_len = bucket_order.shape
    heads = log_sums.shape[1]
    units = rounds * heads
    assert tok_dev == BLOCK and devices % units == 0 and rounds == 2
    split = devices // units
    chips = devices // rounds
    depth = width // heads
    queries = seq_len // tok_dev // split
    held = queries if split == 1 else queries + 1
    capacity = 5 * tok_dev // (4 * devices)
    stride = -(-capacity // 8) * 8
    grad_scale = 1.0 / math.sqrt(seq_len)
    share = width // devices
    dma = pltpu.SemaphoreType.DMA
    hbm, vmem = pl.ANY, pltpu.VMEM

    def low(*shape):
        return pltpu.VMEM(shape, BF16)

    def full(*shape):
        return pltpu.VMEM(shape, F32)

    results = pl.pallas_call(
        functools.partial(core_kernel, heads, stride, split, grad_scale),
        out_shape=[
            low(tok_dev, width),
            full(1, 128),
            full(2, share, width),
        ],
        in_specs=[pl.BlockSpec(memory_space=pl.ANY)] * 7,
        out_specs=whole(3),
        scratch_shapes=[
            full(1, width),
            pltpu.VMEM((rounds, seq_len), jnp.int32),
            full(rounds, heads, tok_dev),
            low(tok_dev, width),
            low(2, width, width),
            low(rounds, tok_dev, width),
            low(3, heads, tok_dev, depth),
            low(3, rounds, chips, tok_dev, depth),
            full(units, 1, tok_dev),
            full(devices, 1, tok_dev),
            low(devices, held, stride, tok_dev),
            low(held, devices * stride, tok_dev),
            low(devices, held, stride, depth),
            *[low(queries + 2, tok_dev, depth)] * 4,
            low(queries + 2, 2 * tok_dev, tok_dev),
            full(queries + 2, tok_dev, depth),
            low(rounds - 1, chips, tok_dev, depth),
            low(2, rounds - 1, chips, tok_dev, depth),
            *[low(2, chips, tok_dev, depth)] * 2,
            low(2, rounds * tok_dev, width // 2),
            full(rounds, tok_dev, width),
            *[low(tok_dev, width)] * 2,
            full(rounds, share, width),
            full(share, width),
            *[full(devices, 8, 128)] * 2,
            low(2, chips, width // chips, width // 2),
            low(2, chips - 1, width // chips, width // 2),
            low(2, chips // 2, width // chips, width // 2),
            dma((heads,)),
            dma((6,)),
            dma((3, chips - 1, 2)),
            dma((3, rounds - 1, chips, 2)),
            dma((devices - 1, 2)),
            dma((2, rounds - 1, chips, 2)),
            dma((2, chips)),
            dma((chips, rounds)),
            dma((devices - 1, 2)),
            dma((2, 2, chips - 1, 2)),
            dma((4, 2)),
        ],
        compiler_params=pltpu.CompilerParams(
            vmem_limit_bytes=VMEM_LIMIT, collective_id=0, has_side_effects=True
        ),
        name="core",
    )(norm_gain.reshape(1, width), bucket_order, log_sums, tokens, cotangent, w_qk, w_v)
    d_tokens, d_gain, d_qk, d_v = pl.pallas_call(
        functools.partial(hand_over, share),
        out_shape=[
            jax.ShapeDtypeStruct((tok_dev, width), BF16),
            jax.ShapeDtypeStruct((1, share), F32),
            jax.ShapeDtypeStruct((share, width), F32),
            jax.ShapeDtypeStruct((share, width), F32),
        ],
        in_specs=whole(3),
        out_specs=[pl.BlockSpec(memory_space=space) for space in (hbm, vmem, hbm, hbm)],
        scratch_shapes=[dma((3,))],
        name="hand_over",
    )(*[pltpu.with_memory_space_constraint(result, vmem) for result in results])
    return (d_tokens, d_gain.reshape(share), d_qk, d_v)


def solution(mesh):
    in_specs = (
        P(("groups", "tok"), None),
        P(),
        P(),
        P(),
        P(("groups", "tok"), None),
        P(None, None, ("groups", "tok")),
        P(None, "groups"),
        P(None, ("groups", "tok")),
    )
    out_specs = (
        P(("groups", "tok"), None),
        P(("groups", "tok")),
        P(("groups", "tok"), None),
        P(("groups", "tok"), None),
    )
    return jax.shard_map(
        per_device, mesh=mesh, in_specs=in_specs, out_specs=out_specs, check_vma=False
    )
```

```python
import functools
import math

import jax
import jax.numpy as jnp
from jax import lax
from jax.experimental import pallas as pl
from jax.experimental.pallas import tpu as pltpu
from jax.sharding import PartitionSpec as P

BLOCK = 256
EPS = 1e-06
VMEM_LIMIT = 62 * 1024 * 1024
MESH = pl.DeviceIdType.MESH
F32 = jnp.float32
BF16 = jnp.bfloat16


def whole(count):
    return [pl.BlockSpec(memory_space=pltpu.VMEM)] * count


def dot_nn(a, b):
    return lax.dot_general(a, b, (((1,), (0,)), ((), ())), preferred_element_type=F32)


def dot_nt(a, b):
    return lax.dot_general(a, b, (((1,), (1,)), ((), ())), preferred_element_type=F32)


def dot_tn(a, b):
    return lax.dot_general(a, b, (((0,), (0,)), ((), ())), preferred_element_type=F32)


def slot_row(order, tok_dev, stride):
    size = order.shape[1]
    owner = lax.div(order, jnp.int32(tok_dev))
    owner_col = jnp.broadcast_to(owner, (size, size)).T
    before = lax.broadcasted_iota(jnp.int32, (size, size), 0) < lax.broadcasted_iota(
        jnp.int32, (size, size), 1
    )
    earlier = (owner_col == owner) & before
    rank = jnp.sum(earlier.astype(F32), axis=0, keepdims=True).astype(jnp.int32)
    return owner * stride + rank


def one_hot_rows(slots, slot_count):
    size = slots.shape[1]
    ids = lax.broadcasted_iota(jnp.int32, (slot_count, size), 0)
    return jnp.where(ids == slots, 1.0, 0.0).astype(BF16)


def normal_of(x, gain):
    return (x * lax.rsqrt(jnp.mean(x * x, axis=-1, keepdims=True) + EPS) * gain).astype(BF16)


def unit_of(q):
    depth = q.shape[-1]
    scale = lax.rsqrt(jnp.mean(q * q, axis=-1, keepdims=True) + EPS)
    return (q * scale / math.sqrt(depth)).astype(BF16)


def flipped(index, mask):
    bit = 1
    while bit <= mask:
        if mask & bit:
            index = index + bit * (1 - 2 * lax.rem(lax.div(index, bit), 2))
        bit *= 2
    return index


def forwarding_order(masks):
    return sorted(masks, key=lambda m: int(bin(m)[:1:-1].ljust(16, "0"), 2), reverse=True)


def looped(count, unroll, body):
    steps = count // unroll

    def step(i, carry):
        for u in range(unroll):
            body(i * unroll + u)
        return carry

    if steps > 1:
        lax.fori_loop(0, steps, step, 0)
    for i in range(steps * unroll if steps > 1 else 0, count):
        body(i)


def core_kernel(heads, stride, split, grad_scale, *refs):
    gain_hbm, order_hbm, sums_hbm, tokens_hbm, cot_hbm, qk_hbm, v_hbm = refs[:7]
    d_tokens_ref, d_gain_ref, d_weights_ref = refs[7:10]
    (
        gain_ref, order_ref, sums_ref, tokens_ref, maps,
        normal, slab_out, slab_in, sums_out, sums_in_rows, spread, pick, bucket,
        sorted_q, sorted_k, sorted_g, sorted_v, probs, d_query,
        part_out, part_in, home_out, home_in, grads, rows_kept, rows_out, rows_in, ends, ends_in,
        gain_out, gain_back, weights, sums_in, sums_run,
        cot_sem, load_sem, slab_sem, relay_sem, rows_sem, part_sem, home_send_sem,
        home_recv_sem, gain_sem, sums_sem, pair_sem,
    ) = refs[10:]
    devices = lax.axis_size("tok")
    me = lax.axis_index("tok")
    rounds, seq_len = order_ref.shape
    rows, width = tokens_ref.shape
    depth = width // heads
    chips = devices // rounds
    chip, lane = lax.div(me, rounds), lax.rem(me, rounds)
    blocks = seq_len // rows
    queries = blocks // split
    first = lax.rem(chip, split) * queries
    base = 1 if split == 1 else 0
    held = queries + 1 - base
    slot_count = devices * stride
    parts = [slice(head * depth, (head + 1) * depth) for head in range(heads)]

    def remote(src, dst, sems, peer):
        return pltpu.make_async_remote_copy(
            src_ref=src,
            dst_ref=dst,
            send_sem=sems.at[0],
            recv_sem=sems.at[1],
            device_id={"tok": peer},
            device_id_type=MESH,
        )

    barrier = pltpu.get_barrier_semaphore()
    for step in range(1, devices):
        peer = lax.rem(me + step, devices)
        pl.semaphore_signal(barrier, inc=1, device_id={"tok": peer}, device_id_type=MESH)
    cot_loads = [
        pltpu.make_async_copy(cot_hbm.at[:, part], slab_out.at[1, head], cot_sem.at[head])
        for head, part in enumerate(parts)
    ]
    loads = {
        name: pltpu.make_async_copy(src, dst, load_sem.at[place])
        for place, (name, src, dst) in enumerate(
            [
                ("sums", sums_hbm, sums_ref),
                ("tokens", tokens_hbm, tokens_ref),
                ("gain", gain_hbm, gain_ref),
                ("qk", qk_hbm, maps.at[1]),
                ("v", v_hbm, maps.at[0]),
                ("order", order_hbm, order_ref),
            ]
        )
    }
    for name in ("tokens", "gain", "qk", "sums"):
        loads[name].start()

    def chip_at(step):
        return flipped(chip, step)

    def lane_at(step):
        return lax.rem(lane + step, rounds)

    def lane_behind(step):
        return lax.rem(lane + rounds - step, rounds)

    slabs = [
        {
            step: remote(
                slab_out.at[t, lax.div(chip_at(step), split)],
                slab_in.at[t, lane, chip],
                slab_sem.at[t, step - 1],
                chip_at(step) * rounds + lane,
            )
            for step in range(1, chips)
        }
        for t in range(3)
    ]
    relays = [
        {
            (d, step): remote(
                slab_in.at[t, lane, chip_at(step)],
                slab_in.at[t, lane, chip_at(step)],
                relay_sem.at[t, d - 1, step],
                chip * rounds + lane_at(d),
            )
            for d in range(1, rounds)
            for step in range(chips)
        }
        for t in range(3)
    ]
    row_sums = []
    for step in range(1, devices):
        peer = lax.rem(me + step, devices)
        unit = lax.div(lax.div(peer, rounds), split) * rounds + lax.rem(peer, rounds)
        row_sums.append(remote(sums_out.at[unit], sums_in_rows.at[me], rows_sem.at[step - 1], peer))
    shares = [
        {
            (d, step): remote(
                part_out.at[d - 1, chip_at(step)],
                part_in.at[t, d - 1, chip_at(step)],
                part_sem.at[t, d - 1, step],
                chip * rounds + lane_at(d),
            )
            for d in range(1, rounds)
            for step in range(chips)
        }
        for t in range(2)
    ]
    homes = [
        [
            pltpu.make_async_remote_copy(
                src_ref=home_out.at[t, chip_at(step)],
                dst_ref=home_in.at[lane, chip],
                send_sem=home_send_sem.at[t, step],
                recv_sem=home_recv_sem.at[step, lane],
                device_id={"tok": chip_at(step) * rounds + t},
                device_id_type=MESH,
            )
            for step in range(chips)
        ]
        for t in range(2)
    ]
    comings = [
        [
            pltpu.make_async_remote_copy(
                src_ref=home_out.at[0, chip_at(step)],
                dst_ref=home_in.at[l, chip_at(step)],
                send_sem=home_send_sem.at[0, step],
                recv_sem=home_recv_sem.at[step, l],
                device_id={"tok": chip * rounds + 1 - lane},
                device_id_type=MESH,
            )
            for l in range(rounds)
        ]
        for step in range(chips)
    ]
    other = 1 - lane
    sibling = chip * rounds + other
    normal_copy = remote(normal.at[lane], normal.at[lane], pair_sem.at[0], sibling)
    rows_copy = remote(rows_out, rows_in, pair_sem.at[1], sibling)
    gains = []
    for step in range(1, devices):
        peer = lax.rem(me + step, devices)
        gains.append(remote(gain_out.at[peer], gain_back.at[me], gain_sem.at[step - 1], peer))

    bits = chips.bit_length() - 1
    first_slot = [chips - (chips >> k) for k in range(bits)]
    top = lax.div(chip, chips // 2)
    half_width = width // 2
    y_first, y_late = list(range(bits)), [*range(1, bits - 1), 0, bits - 1]
    late_start = 3 * half_width // 4
    sections = [(y_first, slice(0, late_start)), (y_late, slice(late_start, half_width))]

    def half_start(group):
        return pl.multiple_of(half_width * (top + group - 2 * top * group), half_width)

    def physical(bit_order, mask):
        return sum(1 << bit_order[k] for k in range(bits) if mask >> k & 1)

    def sums_copy(group, place, k, mask):
        bit_order, columns = sections[place]
        slot = first_slot[k] + (mask >> (k + 1))
        if k == 0:
            source = weights.at[group, flipped(chip, physical(bit_order, mask)), :, columns]
        else:
            source = sums_run.at[group, mask >> 1, :, columns]
        landing = group if k < bits - 1 else 1 - group
        return pltpu.make_async_remote_copy(
            src_ref=source,
            dst_ref=sums_in.at[landing, slot, :, columns],
            send_sem=sums_sem.at[group, place, slot, 0],
            recv_sem=sums_sem.at[landing, place, slot, 1],
            device_id={"tok": flipped(chip, 1 << bit_order[k]) * rounds + lane},
            device_id_type=MESH,
        )

    stages = [
        [
            [
                {m: sums_copy(group, p, k, m) for m in range(1 << k, chips, 2 << k)}
                for p in range(len(sections))
            ]
            for group in range(2)
        ]
        for k in range(bits)
    ]
    end_copies = [
        remote(
            ends.at[other, :, pl.ds(half_start(group), half_width)],
            ends_in.at[:, pl.ds(half_start(group), half_width)],
            pair_sem.at[2 + group],
            sibling,
        )
        for group in range(2)
    ]
    far_first = sorted(range(1, chips), key=lambda step: (-step.bit_length(), step))
    near_first = list(range(1, chips))

    def send_slabs(t):
        for step in far_first:
            slabs[t][step].start()
        slab_in[t, lane, chip] = slab_out[t, lax.div(chip, split)]

    with jax.named_scope("first"):
        loads["tokens"].wait()
        loads["gain"].wait()
        rows_now = normal_of(tokens_ref[...].astype(F32), gain_ref[...])
        normal[lane] = rows_now
        loads["qk"].wait()
        for load in cot_loads:
            load.start()
        for name in ("v", "order"):
            loads[name].start()
        query = dot_nn(rows_now, maps[1]).astype(BF16)
        for head, part in enumerate(parts):
            slab_out[0, head] = query[:, part]
        loads["sums"].wait()
        for hashing in range(rounds):
            for head in range(heads):
                sums_out[head * rounds + hashing] = sums_ref[hashing, head : head + 1, :]
    with jax.named_scope("barrier"):
        pl.semaphore_wait(barrier, devices - 1)
    with jax.named_scope("sends"):
        for copy in row_sums:
            copy.start()
        send_slabs(0)
        own_unit = lax.div(chip, split) * rounds + lane
        sums_in_rows[me] = sums_out[own_unit]
        for load in cot_loads:
            load.wait()
        send_slabs(1)
        loads["v"].wait()
        value = dot_nn(normal[lane], maps[0]).astype(BF16)
        for head, part in enumerate(parts):
            slab_out[2, head] = value[:, part]
        send_slabs(2)
        normal_copy.start()
        for t in range(3):
            for d in range(1, rounds):
                relays[t][d, 0].start()
        loads["order"].wait()

    token_ids = lax.broadcasted_iota(jnp.int32, (rows, rows), 0)

    def tables(place):
        block = lax.rem(first + (place + base - 1 + blocks), blocks)
        start = pl.multiple_of(block * rows, rows)
        order = order_ref[pl.ds(lane, 1), pl.ds(start, rows)]
        chosen = one_hot_rows(slot_row(order, rows, stride), slot_count)
        pick[place] = chosen
        within = jnp.where(token_ids == lax.rem(order, jnp.int32(rows)), 1.0, 0.0).astype(BF16)
        moved = dot_nt(chosen, within).astype(BF16)
        spread[:, place] = moved.reshape(devices, stride, rows)

    with jax.named_scope("tables"):
        looped(held, 4, tables)

    def bucket_rows(t, source_chip, source_lane):
        source = source_chip * rounds + source_lane
        table = spread[source].reshape(held * stride, rows)
        placed = dot_nn(table, slab_in[t, source_lane, source_chip]).astype(BF16)
        bucket[source] = placed.reshape(held, stride, depth)

    def take_slabs(t):
        with jax.named_scope(f"take{t}"):
            for step in near_first:
                slabs[t][step].wait_recv()
                for d in range(1, rounds):
                    relays[t][d, step].start()

    def gather(t, own=True):
        with jax.named_scope(f"gather{t}"):
            if own:
                looped(chips, 8, lambda place: bucket_rows(t, place, lane))
            for d in range(1, rounds):
                for step in [0, *near_first]:
                    relays[t][d, step].wait_recv()
                looped(chips, 8, lambda place: bucket_rows(t, place, lane_behind(d)))

    def sorted_rows(place):
        data = bucket[:, place].reshape(slot_count, depth)
        return dot_tn(pick[place], data).astype(BF16)

    def sort_queries(place):
        q = sorted_rows(place)
        sorted_q[place + base] = q
        sorted_k[place + base] = unit_of(q.astype(F32))

    def sort_cotangents(place):
        sorted_g[place + base] = sorted_rows(place)

    take_slabs(0)
    gather(0)
    with jax.named_scope("sortq"):
        looped(held, 16, sort_queries)
    if split == 1:
        sorted_k[0] = sorted_k[queries]
    with jax.named_scope("rowsums"):
        for copy in row_sums:
            copy.wait_recv()
    diagonal = lax.broadcasted_iota(jnp.int32, (2 * rows, rows), 0) == rows + (
        lax.broadcasted_iota(jnp.int32, (2 * rows, rows), 1)
    )

    def probabilities(i):
        keys = sorted_k[pl.ds(i, 2)].reshape(2 * rows, depth)
        scores = dot_nt(keys, sorted_q[i + 1]) - sums_in_rows[first + i]
        probs[i + 1] = jnp.where(diagonal, 0.0, jnp.exp(scores)).astype(BF16)

    with jax.named_scope("probs"):
        looped(queries, 8, probabilities)
    if split > 1:
        probs[0] = jnp.zeros((2 * rows, rows), BF16)
        probs[queries + 1] = jnp.zeros((2 * rows, rows), BF16)
        sorted_g[queries + 1] = jnp.zeros((rows, depth), BF16)

    def after(j):
        return lax.rem(j, queries) + 1 if split == 1 else j + 1

    def bucket_back(place):
        placed = dot_nn(pick[place], sorted_v[place + base]).astype(BF16)
        bucket[:, place] = placed.reshape(devices, stride, depth)

    def home_rows(source_chip, source_lane):
        source = source_chip * rounds + source_lane
        table = spread[source].reshape(held * stride, rows)
        return dot_tn(table, bucket[source].reshape(held * stride, depth))

    def send_home(t):
        with jax.named_scope(f"home{t}"):
            if t > 0:
                for copy in shares[t - 1].values():
                    copy.wait_send()
            for d in range(1, rounds):

                def share(place):
                    part_out[d - 1, place] = home_rows(place, lane_at(d)).astype(BF16)

                looped(chips, 8, share)
                for step in [*far_first, 0]:
                    shares[t][d, step].start()

            def keep(place):
                d_query[place] = home_rows(place, lane)

            looped(chips, 8, keep)
            if t == 0:
                take_slabs(2)
                looped(chips, 8, lambda place: bucket_rows(2, place, lane))
            for step in [*far_first, 0]:
                for d in range(1, rounds):
                    shares[t][d, step].wait_recv()
            for place in range(chips):
                total = d_query[place]
                for d in range(1, rounds):
                    total += part_in[t, d - 1, place].astype(F32)
                home_out[t, place] = total.astype(BF16)
            for step in near_first:
                homes[t][step].start()

            @pl.when(lane == t)
            def _():
                home_in[lane, chip] = home_out[t, chip]

            @pl.when(lane != t)
            def _():
                homes[t][0].start()


    def value_gradients(place):
        j = place + base
        grad = dot_nn(probs[j, rows:, :], sorted_g[j])
        grad += dot_nn(probs[after(j), :rows, :], sorted_g[after(j)])
        sorted_v[j] = grad.astype(BF16)

    take_slabs(1)
    gather(1)
    with jax.named_scope("sortg"):
        looped(held, 16, sort_cotangents)
    with jax.named_scope("dv"):
        looped(held, 16, value_gradients)
        looped(held, 16, bucket_back)
    send_home(0)
    gather(2, own=False)

    def sort_values(place):
        sorted_v[place + base] = sorted_rows(place)

    with jax.named_scope("sortv"):
        looped(held, 16, sort_values)
    if split == 1:
        sorted_v[0] = sorted_v[queries]
    else:
        d_query[0] = jnp.zeros((rows, depth), F32)
        sorted_q[queries + 1] = jnp.zeros((rows, depth), BF16)

    def score_gradients(i):
        j = i + 1
        values = sorted_v[pl.ds(i, 2)].reshape(2 * rows, depth)
        w = probs[j].astype(F32)
        d_probs = dot_nt(values, sorted_g[j])
        delta = jnp.sum(w * d_probs, axis=0, keepdims=True)
        probs[j] = (w * (d_probs - delta)).astype(BF16)

    def query_gradients(i):
        keys = sorted_k[pl.ds(i, 2)].reshape(2 * rows, depth)
        d_query[i + 1] = dot_tn(probs[i + 1], keys)

    def key_gradients(place):
        j = place + base
        q = sorted_q[j].astype(F32)
        dk = dot_nn(probs[j, rows:, :], sorted_q[j])
        dk += dot_nn(probs[after(j), :rows, :], sorted_q[after(j)])
        scale = lax.rsqrt(jnp.mean(q * q, axis=-1, keepdims=True) + EPS)
        along = jnp.mean(q * dk, axis=-1, keepdims=True)
        pulled = (dk * scale - q * (scale * scale * scale * along)) / math.sqrt(depth)
        sorted_v[j] = (d_query[j] + pulled).astype(BF16)

    def assemble(group):
        steps = [m for m in range(chips) if (m.bit_length() == bits) == (group == 1)]
        with jax.named_scope(f"wait_home{group}"):
            for step in steps:
                if step > 0:
                    for coming in comings[step]:
                        coming.wait_recv()
                else:
                    pltpu.make_async_remote_copy(
                        src_ref=home_out.at[0, chip],
                        dst_ref=home_in.at[other, chip],
                        send_sem=home_send_sem.at[0, 0],
                        recv_sem=home_recv_sem.at[0, other],
                        device_id={"tok": sibling},
                        device_id_type=MESH,
                    ).wait_recv()
        half_heads = heads // 2
        start = half_heads * (top + group - 2 * top * group)
        for l in range(rounds):
            for place in range(half_heads):
                total = home_in[l, (start + place) * split]
                for p in range(1, split):
                    more = home_in[l, (start + place) * split + p]
                    total = (total.astype(F32) + more.astype(F32)).astype(BF16)
                grads[group, l * rows : (l + 1) * rows, parts[place]] = total

    def weight_gradient(group):
        with jax.named_scope(f"weight{group}"):
            normals = normal[...].reshape(rounds * rows, width)
            grad = dot_tn(normals, grads[group]) * grad_scale
            weights[group] = grad.astype(BF16).reshape(chips, width // chips, half_width)
            for copies in stages[0][group]:
                for mask in forwarding_order(copies):
                    copies[mask].start()

    def row_gradients(group):
        with jax.named_scope(f"rowgrad{group}"):
            columns = pl.ds(half_start(group), half_width)
            for l in range(rounds):
                part = dot_nt(grads[group, l * rows : (l + 1) * rows], maps[lane, :, columns])
                if group == 0:
                    rows_kept[l] = part
                else:
                    rows_kept[l] += part

    def run_sums(k, group):
        waiting = []
        with jax.named_scope(f"sum{k}_{group}"):
            for mask in forwarding_order(stages[k][group][0]):
                for place, (bit_order, columns) in enumerate(sections):
                    rest = mask - (1 << k)
                    sender = group if k < bits - 1 else 1 - group
                    stages[k][sender][place][mask].wait_recv()
                    slot = first_slot[k] + (mask >> (k + 1))
                    came = sums_in[group, slot, :, columns].astype(F32)
                    if k == 0:
                        row = flipped(chip, physical(bit_order, rest))
                        before = weights[group, row, :, columns]
                    else:
                        before = sums_run[group, rest >> 1, :, columns]
                    run = before.astype(F32) + came
                    if k == bits - 1:
                        column = pl.multiple_of(half_start(group) + columns.start, 128)
                        into = pl.ds(column, columns.stop - columns.start)
                        for l in range(rounds):
                            ends[l, :, into] = run[l * share : (l + 1) * share]
                        continue
                    sums_run[group, rest >> 1, :, columns] = run.astype(BF16)
                    waiting.append(stages[k + 1][group][place].get(rest))
                    if len(waiting) > 1:
                        onward = waiting.pop(0)
                        if onward is not None:
                            onward.start()
            for onward in waiting:
                if onward is not None:
                    onward.start()
            if k == bits - 1:
                end_copies[group].start()

    share = width // devices
    with jax.named_scope("ds"):
        looped(queries, 16, score_gradients)
    with jax.named_scope("dq"):
        looped(queries, 16, query_gradients)
    with jax.named_scope("dk"):
        looped(held, 16, key_gradients)
    with jax.named_scope("back"):
        looped(held, 16, bucket_back)
    send_home(1)
    normal_copy.wait_recv()
    assemble(0)
    weight_gradient(0)
    row_gradients(0)
    run_sums(0, 0)
    assemble(1)
    weight_gradient(1)
    row_gradients(1)
    rows_out[...] = rows_kept[other].astype(BF16)
    rows_copy.start()
    for k in range(1, bits - 1):
        run_sums(k, 0)
        run_sums(k - 1, 1)
    rows_copy.wait_recv()
    d_normal = rows_kept[lane] + rows_in[...].astype(F32)
    with jax.named_scope("rows"):
        x = tokens_ref[...].astype(F32)
        scale = lax.rsqrt(jnp.mean(x * x, axis=-1, keepdims=True) + EPS)
        gain_total = jnp.sum(d_normal * (x * scale), axis=0, keepdims=True) * grad_scale
        share = width // devices
        gain_out[...] = jnp.zeros(gain_out.shape, F32)
        for device in range(devices):
            gain_out[device, 0:1, 0:share] = gain_total[:, device * share : (device + 1) * share]
        gain_back[me] = gain_out[me]
        for copy in gains:
            copy.start()
        t = d_normal * gain_ref[...]
        along = jnp.mean(x * t, axis=-1, keepdims=True)
        d_tokens_ref[...] = (t * scale - x * (scale * scale * scale * along)).astype(BF16)

    run_sums(bits - 2, 1)
    run_sums(bits - 1, 0)
    run_sums(bits - 1, 1)
    with jax.named_scope("ends"):
        d_weights_ref[lane] = ends[lane]
        for copy in end_copies:
            copy.wait_recv()
        d_weights_ref[other] = ends_in[...]
    with jax.named_scope("sendwaits"):
        for copy in gains:
            copy.wait_recv()
        d_gain_ref[...] = jnp.sum(gain_back[:, 0, :], axis=0, keepdims=True)
        for stage in stages:
            for copies in [*stage[0], *stage[1]]:
                for copy in copies.values():
                    copy.wait_send()
        for group in [*slabs, *relays, shares[-1]]:
            for copy in group.values():
                copy.wait_send()
        for t in range(2):
            for step in range(1, chips):
                homes[t][step].wait_send()
        pltpu.make_async_remote_copy(
            src_ref=home_out.at[0, chip],
            dst_ref=home_in.at[lane, chip],
            send_sem=home_send_sem.at[other, 0],
            recv_sem=home_recv_sem.at[0, lane],
            device_id={"tok": sibling},
            device_id_type=MESH,
        ).wait_send()
        for copy in [*row_sums, *gains, normal_copy, rows_copy, *end_copies]:
            copy.wait_send()


def hand_over(share, d_tokens_in, d_gain_in, d_weights_in, d_tokens, d_gain, d_qk, d_v, sems):
    pairs = [
        (d_tokens_in, d_tokens), (d_weights_in.at[1], d_qk), (d_weights_in.at[0], d_v)
    ]
    copies = [pltpu.make_async_copy(*pair, sems.at[i]) for i, pair in enumerate(pairs)]
    for copy in copies:
        copy.start()
    d_gain[...] = d_gain_in[:, :share]
    for copy in copies:
        copy.wait()


def per_device(tokens, norm_gain, w_qk, w_v, cotangent, log_sums, bucket_order, token_position):
    devices = lax.axis_size("tok")
    tok_dev, width = tokens.shape
    rounds, seq_len = bucket_order.shape
    heads = log_sums.shape[1]
    units = rounds * heads
    assert tok_dev == BLOCK and devices % units == 0 and rounds == 2
    split = devices // units
    chips = devices // rounds
    depth = width // heads
    queries = seq_len // tok_dev // split
    held = queries if split == 1 else queries + 1
    capacity = 5 * tok_dev // (4 * devices)
    stride = -(-capacity // 8) * 8
    grad_scale = 1.0 / math.sqrt(seq_len)
    share = width // devices
    dma = pltpu.SemaphoreType.DMA
    hbm, vmem = pl.ANY, pltpu.VMEM

    def low(*shape):
        return pltpu.VMEM(shape, BF16)

    def full(*shape):
        return pltpu.VMEM(shape, F32)

    results = pl.pallas_call(
        functools.partial(core_kernel, heads, stride, split, grad_scale),
        out_shape=[
            low(tok_dev, width),
            full(1, 128),
            full(2, share, width),
        ],
        in_specs=[pl.BlockSpec(memory_space=pl.ANY)] * 7,
        out_specs=whole(3),
        scratch_shapes=[
            full(1, width),
            pltpu.VMEM((rounds, seq_len), jnp.int32),
            full(rounds, heads, tok_dev),
            low(tok_dev, width),
            low(2, width, width),
            low(rounds, tok_dev, width),
            low(3, heads, tok_dev, depth),
            low(3, rounds, chips, tok_dev, depth),
            full(units, 1, tok_dev),
            full(devices, 1, tok_dev),
            low(devices, held, stride, tok_dev),
            low(held, devices * stride, tok_dev),
            low(devices, held, stride, depth),
            *[low(queries + 2, tok_dev, depth)] * 4,
            low(queries + 2, 2 * tok_dev, tok_dev),
            full(queries + 2, tok_dev, depth),
            low(rounds - 1, chips, tok_dev, depth),
            low(2, rounds - 1, chips, tok_dev, depth),
            *[low(2, chips, tok_dev, depth)] * 2,
            low(2, rounds * tok_dev, width // 2),
            full(rounds, tok_dev, width),
            *[low(tok_dev, width)] * 2,
            full(rounds, share, width),
            full(share, width),
            *[full(devices, 8, 128)] * 2,
            low(2, chips, width // chips, width // 2),
            low(2, chips - 1, width // chips, width // 2),
            low(2, chips // 2, width // chips, width // 2),
            dma((heads,)),
            dma((6,)),
            dma((3, chips - 1, 2)),
            dma((3, rounds - 1, chips, 2)),
            dma((devices - 1, 2)),
            dma((2, rounds - 1, chips, 2)),
            dma((2, chips)),
            dma((chips, rounds)),
            dma((devices - 1, 2)),
            dma((2, 2, chips - 1, 2)),
            dma((4, 2)),
        ],
        compiler_params=pltpu.CompilerParams(
            vmem_limit_bytes=VMEM_LIMIT, collective_id=0, has_side_effects=True
        ),
        name="core",
    )(norm_gain.reshape(1, width), bucket_order, log_sums, tokens, cotangent, w_qk, w_v)
    d_tokens, d_gain, d_qk, d_v = pl.pallas_call(
        functools.partial(hand_over, share),
        out_shape=[
            jax.ShapeDtypeStruct((tok_dev, width), BF16),
            jax.ShapeDtypeStruct((1, share), F32),
            jax.ShapeDtypeStruct((share, width), F32),
            jax.ShapeDtypeStruct((share, width), F32),
        ],
        in_specs=whole(3),
        out_specs=[pl.BlockSpec(memory_space=space) for space in (hbm, vmem, hbm, hbm)],
        scratch_shapes=[dma((3,))],
        name="hand_over",
    )(*[pltpu.with_memory_space_constraint(result, vmem) for result in results])
    return (d_tokens, d_gain.reshape(share), d_qk, d_v)


def solution(mesh):
    in_specs = (
        P(("groups", "tok"), None),
        P(),
        P(),
        P(),
        P(("groups", "tok"), None),
        P(None, None, ("groups", "tok")),
        P(None, "groups"),
        P(None, ("groups", "tok")),
    )
    out_specs = (
        P(("groups", "tok"), None),
        P(("groups", "tok")),
        P(("groups", "tok"), None),
        P(("groups", "tok"), None),
    )
    return jax.shard_map(
        per_device, mesh=mesh, in_specs=in_specs, out_specs=out_specs, check_vma=False
    )
```

```python
import functools
import math

import jax
import jax.numpy as jnp
from jax import lax
from jax.experimental import pallas as pl
from jax.experimental.pallas import tpu as pltpu
from jax.sharding import PartitionSpec as P

BLOCK = 256
EPS = 1e-06
VMEM_LIMIT = 62 * 1024 * 1024
MESH = pl.DeviceIdType.MESH
F32 = jnp.float32
BF16 = jnp.bfloat16


def whole(count):
    return [pl.BlockSpec(memory_space=pltpu.VMEM)] * count


def dot_nn(a, b):
    return lax.dot_general(a, b, (((1,), (0,)), ((), ())), preferred_element_type=F32)


def dot_nt(a, b):
    return lax.dot_general(a, b, (((1,), (1,)), ((), ())), preferred_element_type=F32)


def dot_tn(a, b):
    return lax.dot_general(a, b, (((0,), (0,)), ((), ())), preferred_element_type=F32)


def slot_row(order, tok_dev, stride):
    size = order.shape[1]
    owner = lax.div(order, jnp.int32(tok_dev))
    owner_col = jnp.broadcast_to(owner, (size, size)).T
    before = lax.broadcasted_iota(jnp.int32, (size, size), 0) < lax.broadcasted_iota(
        jnp.int32, (size, size), 1
    )
    earlier = (owner_col == owner) & before
    rank = jnp.sum(earlier.astype(F32), axis=0, keepdims=True).astype(jnp.int32)
    return owner * stride + rank


def one_hot_rows(slots, slot_count):
    size = slots.shape[1]
    ids = lax.broadcasted_iota(jnp.int32, (slot_count, size), 0)
    return jnp.where(ids == slots, 1.0, 0.0).astype(BF16)


def normal_of(x, gain):
    return (x * lax.rsqrt(jnp.mean(x * x, axis=-1, keepdims=True) + EPS) * gain).astype(BF16)


def unit_of(q):
    depth = q.shape[-1]
    scale = lax.rsqrt(jnp.mean(q * q, axis=-1, keepdims=True) + EPS)
    return (q * scale / math.sqrt(depth)).astype(BF16)


def flipped(index, mask):
    bit = 1
    while bit <= mask:
        if mask & bit:
            index = index + bit * (1 - 2 * lax.rem(lax.div(index, bit), 2))
        bit *= 2
    return index


def forwarding_order(masks):
    return sorted(masks, key=lambda m: int(bin(m)[:1:-1].ljust(16, "0"), 2), reverse=True)


def looped(count, unroll, body):
    steps = count // unroll

    def step(i, carry):
        for u in range(unroll):
            body(i * unroll + u)
        return carry

    if steps > 1:
        lax.fori_loop(0, steps, step, 0)
    for i in range(steps * unroll if steps > 1 else 0, count):
        body(i)


def core_kernel(heads, stride, split, grad_scale, *refs):
    gain_hbm, order_hbm, sums_hbm, tokens_hbm, cot_hbm, qk_hbm, v_hbm = refs[:7]
    d_tokens_ref, d_gain_ref, d_weights_ref = refs[7:10]
    (
        gain_ref, order_ref, sums_ref, tokens_ref, maps,
        normal, slab_out, slab_in, sums_out, sums_in_rows, spread, pick, bucket,
        sorted_q, sorted_k, sorted_g, sorted_v, probs, d_query,
        part_out, part_in, home_out, home_in, grads, rows_kept, rows_out, rows_in, ends, ends_in,
        gain_out, gain_back, weights, sums_in, sums_run,
        cot_sem, load_sem, slab_sem, relay_sem, rows_sem, part_sem, home_send_sem,
        home_recv_sem, gain_sem, sums_sem, pair_sem,
    ) = refs[10:]
    devices = lax.axis_size("tok")
    me = lax.axis_index("tok")
    rounds, seq_len = order_ref.shape
    rows, width = tokens_ref.shape
    depth = width // heads
    chips = devices // rounds
    chip, lane = lax.div(me, rounds), lax.rem(me, rounds)
    blocks = seq_len // rows
    queries = blocks // split
    first = lax.rem(chip, split) * queries
    base = 1 if split == 1 else 0
    held = queries + 1 - base
    slot_count = devices * stride
    parts = [slice(head * depth, (head + 1) * depth) for head in range(heads)]

    def remote(src, dst, sems, peer):
        return pltpu.make_async_remote_copy(
            src_ref=src,
            dst_ref=dst,
            send_sem=sems.at[0],
            recv_sem=sems.at[1],
            device_id={"tok": peer},
            device_id_type=MESH,
        )

    barrier = pltpu.get_barrier_semaphore()
    for step in range(1, devices):
        peer = lax.rem(me + step, devices)
        pl.semaphore_signal(barrier, inc=1, device_id={"tok": peer}, device_id_type=MESH)
    cot_loads = [
        pltpu.make_async_copy(cot_hbm.at[:, part], slab_out.at[1, head], cot_sem.at[head])
        for head, part in enumerate(parts)
    ]
    loads = {
        name: pltpu.make_async_copy(src, dst, load_sem.at[place])
        for place, (name, src, dst) in enumerate(
            [
                ("sums", sums_hbm, sums_ref),
                ("tokens", tokens_hbm, tokens_ref),
                ("gain", gain_hbm, gain_ref),
                ("qk", qk_hbm, maps.at[1]),
                ("v", v_hbm, maps.at[0]),
                ("order", order_hbm, order_ref),
            ]
        )
    }
    for name in ("tokens", "gain", "qk", "sums"):
        loads[name].start()

    def chip_at(step):
        return flipped(chip, step)

    def lane_at(step):
        return lax.rem(lane + step, rounds)

    def lane_behind(step):
        return lax.rem(lane + rounds - step, rounds)

    slabs = [
        {
            step: remote(
                slab_out.at[t, lax.div(chip_at(step), split)],
                slab_in.at[t, lane, chip],
                slab_sem.at[t, step - 1],
                chip_at(step) * rounds + lane,
            )
            for step in range(1, chips)
        }
        for t in range(3)
    ]
    relays = [
        {
            (d, step): remote(
                slab_in.at[t, lane, chip_at(step)],
                slab_in.at[t, lane, chip_at(step)],
                relay_sem.at[t, d - 1, step],
                chip * rounds + lane_at(d),
            )
            for d in range(1, rounds)
            for step in range(chips)
        }
        for t in range(3)
    ]
    row_sums = []
    for step in range(1, devices):
        peer = lax.rem(me + step, devices)
        unit = lax.div(lax.div(peer, rounds), split) * rounds + lax.rem(peer, rounds)
        row_sums.append(remote(sums_out.at[unit], sums_in_rows.at[me], rows_sem.at[step - 1], peer))
    shares = [
        {
            (d, step): remote(
                part_out.at[d - 1, chip_at(step)],
                part_in.at[t, d - 1, chip_at(step)],
                part_sem.at[t, d - 1, step],
                chip * rounds + lane_at(d),
            )
            for d in range(1, rounds)
            for step in range(chips)
        }
        for t in range(2)
    ]
    homes = [
        [
            pltpu.make_async_remote_copy(
                src_ref=home_out.at[t, chip_at(step)],
                dst_ref=home_in.at[lane, chip],
                send_sem=home_send_sem.at[t, step],
                recv_sem=home_recv_sem.at[step, lane],
                device_id={"tok": chip_at(step) * rounds + t},
                device_id_type=MESH,
            )
            for step in range(chips)
        ]
        for t in range(2)
    ]
    comings = [
        [
            pltpu.make_async_remote_copy(
                src_ref=home_out.at[0, chip_at(step)],
                dst_ref=home_in.at[l, chip_at(step)],
                send_sem=home_send_sem.at[0, step],
                recv_sem=home_recv_sem.at[step, l],
                device_id={"tok": chip * rounds + 1 - lane},
                device_id_type=MESH,
            )
            for l in range(rounds)
        ]
        for step in range(chips)
    ]
    other = 1 - lane
    sibling = chip * rounds + other
    normal_copy = remote(normal.at[lane], normal.at[lane], pair_sem.at[0], sibling)
    rows_copy = remote(rows_out, rows_in, pair_sem.at[1], sibling)
    gains = []
    for step in range(1, devices):
        peer = lax.rem(me + step, devices)
        gains.append(remote(gain_out.at[peer], gain_back.at[me], gain_sem.at[step - 1], peer))

    bits = chips.bit_length() - 1
    first_slot = [chips - (chips >> k) for k in range(bits)]
    top = lax.div(chip, chips // 2)
    half_width = width // 2
    y_first, y_late = list(range(bits)), [*range(1, bits - 1), 0, bits - 1]
    late_start = 3 * half_width // 4
    sections = [(y_first, slice(0, late_start)), (y_late, slice(late_start, half_width))]

    def half_start(group):
        return pl.multiple_of(half_width * (top + group - 2 * top * group), half_width)

    def physical(bit_order, mask):
        return sum(1 << bit_order[k] for k in range(bits) if mask >> k & 1)

    def sums_copy(group, place, k, mask):
        bit_order, columns = sections[place]
        slot = first_slot[k] + (mask >> (k + 1))
        if k == 0:
            source = weights.at[group, flipped(chip, physical(bit_order, mask)), :, columns]
        else:
            source = sums_run.at[group, mask >> 1, :, columns]
        landing = group if k < bits - 1 else 1 - group
        return pltpu.make_async_remote_copy(
            src_ref=source,
            dst_ref=sums_in.at[landing, slot, :, columns],
            send_sem=sums_sem.at[group, place, slot, 0],
            recv_sem=sums_sem.at[landing, place, slot, 1],
            device_id={"tok": flipped(chip, 1 << bit_order[k]) * rounds + lane},
            device_id_type=MESH,
        )

    stages = [
        [
            [
                {m: sums_copy(group, p, k, m) for m in range(1 << k, chips, 2 << k)}
                for p in range(len(sections))
            ]
            for group in range(2)
        ]
        for k in range(bits)
    ]
    end_copies = [
        remote(
            ends.at[other, :, pl.ds(half_start(group), half_width)],
            ends_in.at[:, pl.ds(half_start(group), half_width)],
            pair_sem.at[2 + group],
            sibling,
        )
        for group in range(2)
    ]
    far_first = sorted(range(1, chips), key=lambda step: (-step.bit_length(), step))
    near_first = list(range(1, chips))

    def send_slabs(t):
        for step in far_first:
            slabs[t][step].start()
        slab_in[t, lane, chip] = slab_out[t, lax.div(chip, split)]

    with jax.named_scope("first"):
        loads["tokens"].wait()
        loads["gain"].wait()
        rows_now = normal_of(tokens_ref[...].astype(F32), gain_ref[...])
        normal[lane] = rows_now
        loads["qk"].wait()
        for load in cot_loads:
            load.start()
        for name in ("v", "order"):
            loads[name].start()
        query = dot_nn(rows_now, maps[1]).astype(BF16)
        for head, part in enumerate(parts):
            slab_out[0, head] = query[:, part]
        loads["sums"].wait()
        for hashing in range(rounds):
            for head in range(heads):
                sums_out[head * rounds + hashing] = sums_ref[hashing, head : head + 1, :]
    with jax.named_scope("barrier"):
        pl.semaphore_wait(barrier, devices - 1)
    with jax.named_scope("sends"):
        for copy in row_sums:
            copy.start()
        send_slabs(0)
        own_unit = lax.div(chip, split) * rounds + lane
        sums_in_rows[me] = sums_out[own_unit]
        for load in cot_loads:
            load.wait()
        send_slabs(1)
        loads["v"].wait()
        value = dot_nn(normal[lane], maps[0]).astype(BF16)
        for head, part in enumerate(parts):
            slab_out[2, head] = value[:, part]
        send_slabs(2)
        normal_copy.start()
        for t in range(3):
            for d in range(1, rounds):
                relays[t][d, 0].start()
        loads["order"].wait()

    token_ids = lax.broadcasted_iota(jnp.int32, (rows, rows), 0)

    def tables(place):
        block = lax.rem(first + (place + base - 1 + blocks), blocks)
        start = pl.multiple_of(block * rows, rows)
        order = order_ref[pl.ds(lane, 1), pl.ds(start, rows)]
        chosen = one_hot_rows(slot_row(order, rows, stride), slot_count)
        pick[place] = chosen
        within = jnp.where(token_ids == lax.rem(order, jnp.int32(rows)), 1.0, 0.0).astype(BF16)
        moved = dot_nt(chosen, within).astype(BF16)
        spread[:, place] = moved.reshape(devices, stride, rows)

    with jax.named_scope("tables"):
        looped(held, 4, tables)

    def bucket_rows(t, source_chip, source_lane):
        source = source_chip * rounds + source_lane
        table = spread[source].reshape(held * stride, rows)
        placed = dot_nn(table, slab_in[t, source_lane, source_chip]).astype(BF16)
        bucket[source] = placed.reshape(held, stride, depth)

    def take_slabs(t):
        with jax.named_scope(f"take{t}"):
            for step in near_first:
                slabs[t][step].wait_recv()
                for d in range(1, rounds):
                    relays[t][d, step].start()

    def gather(t, own=True):
        with jax.named_scope(f"gather{t}"):
            if own:
                looped(chips, 8, lambda place: bucket_rows(t, place, lane))
            for d in range(1, rounds):
                for step in [0, *near_first]:
                    relays[t][d, step].wait_recv()
                looped(chips, 8, lambda place: bucket_rows(t, place, lane_behind(d)))

    def sorted_rows(place):
        data = bucket[:, place].reshape(slot_count, depth)
        return dot_tn(pick[place], data).astype(BF16)

    def sort_queries(place):
        q = sorted_rows(place)
        sorted_q[place + base] = q
        sorted_k[place + base] = unit_of(q.astype(F32))

    def sort_cotangents(place):
        sorted_g[place + base] = sorted_rows(place)

    take_slabs(0)
    gather(0)
    with jax.named_scope("sortq"):
        looped(held, 16, sort_queries)
    if split == 1:
        sorted_k[0] = sorted_k[queries]
    with jax.named_scope("rowsums"):
        for copy in row_sums:
            copy.wait_recv()
    diagonal = lax.broadcasted_iota(jnp.int32, (2 * rows, rows), 0) == rows + (
        lax.broadcasted_iota(jnp.int32, (2 * rows, rows), 1)
    )

    def probabilities(i):
        keys = sorted_k[pl.ds(i, 2)].reshape(2 * rows, depth)
        scores = dot_nt(keys, sorted_q[i + 1]) - sums_in_rows[first + i]
        probs[i + 1] = jnp.where(diagonal, 0.0, jnp.exp(scores)).astype(BF16)

    with jax.named_scope("probs"):
        looped(queries, 8, probabilities)
    if split > 1:
        probs[0] = jnp.zeros((2 * rows, rows), BF16)
        probs[queries + 1] = jnp.zeros((2 * rows, rows), BF16)
        sorted_g[queries + 1] = jnp.zeros((rows, depth), BF16)

    def after(j):
        return lax.rem(j, queries) + 1 if split == 1 else j + 1

    def bucket_back(place):
        placed = dot_nn(pick[place], sorted_v[place + base]).astype(BF16)
        bucket[:, place] = placed.reshape(devices, stride, depth)

    def home_rows(source_chip, source_lane):
        source = source_chip * rounds + source_lane
        table = spread[source].reshape(held * stride, rows)
        return dot_tn(table, bucket[source].reshape(held * stride, depth))

    def send_home(t):
        with jax.named_scope(f"home{t}"):
            if t > 0:
                for copy in shares[t - 1].values():
                    copy.wait_send()
            for d in range(1, rounds):

                def share(place):
                    part_out[d - 1, place] = home_rows(place, lane_at(d)).astype(BF16)

                looped(chips, 8, share)
                for step in [*far_first, 0]:
                    shares[t][d, step].start()

            def keep(place):
                d_query[place] = home_rows(place, lane)

            looped(chips, 8, keep)
            if t == 0:
                take_slabs(2)
                looped(chips, 8, lambda place: bucket_rows(2, place, lane))
            for step in [*far_first, 0]:
                for d in range(1, rounds):
                    shares[t][d, step].wait_recv()
            for place in range(chips):
                total = d_query[place]
                for d in range(1, rounds):
                    total += part_in[t, d - 1, place].astype(F32)
                home_out[t, place] = total.astype(BF16)
            for step in near_first:
                homes[t][step].start()

            @pl.when(lane == t)
            def _():
                home_in[lane, chip] = home_out[t, chip]

            @pl.when(lane != t)
            def _():
                homes[t][0].start()


    def value_gradients(place):
        j = place + base
        grad = dot_nn(probs[j, rows:, :], sorted_g[j])
        grad += dot_nn(probs[after(j), :rows, :], sorted_g[after(j)])
        sorted_v[j] = grad.astype(BF16)

    take_slabs(1)
    gather(1)
    with jax.named_scope("sortg"):
        looped(held, 16, sort_cotangents)
    with jax.named_scope("dv"):
        looped(held, 16, value_gradients)
        looped(held, 16, bucket_back)
    send_home(0)
    gather(2, own=False)

    def sort_values(place):
        sorted_v[place + base] = sorted_rows(place)

    with jax.named_scope("sortv"):
        looped(held, 16, sort_values)
    if split == 1:
        sorted_v[0] = sorted_v[queries]
    else:
        d_query[0] = jnp.zeros((rows, depth), F32)
        sorted_q[queries + 1] = jnp.zeros((rows, depth), BF16)

    def score_gradients(i):
        j = i + 1
        values = sorted_v[pl.ds(i, 2)].reshape(2 * rows, depth)
        w = probs[j].astype(F32)
        d_probs = dot_nt(values, sorted_g[j])
        delta = jnp.sum(w * d_probs, axis=0, keepdims=True)
        probs[j] = (w * (d_probs - delta)).astype(BF16)

    def query_gradients(i):
        keys = sorted_k[pl.ds(i, 2)].reshape(2 * rows, depth)
        d_query[i + 1] = dot_tn(probs[i + 1], keys)

    def key_gradients(place):
        j = place + base
        q = sorted_q[j].astype(F32)
        dk = dot_nn(probs[j, rows:, :], sorted_q[j])
        dk += dot_nn(probs[after(j), :rows, :], sorted_q[after(j)])
        scale = lax.rsqrt(jnp.mean(q * q, axis=-1, keepdims=True) + EPS)
        along = jnp.mean(q * dk, axis=-1, keepdims=True)
        pulled = (dk * scale - q * (scale * scale * scale * along)) / math.sqrt(depth)
        sorted_v[j] = (d_query[j] + pulled).astype(BF16)

    def assemble(group):
        steps = [m for m in range(chips) if (m.bit_length() == bits) == (group == 1)]
        with jax.named_scope(f"wait_home{group}"):
            for step in steps:
                if step > 0:
                    for coming in comings[step]:
                        coming.wait_recv()
                else:
                    pltpu.make_async_remote_copy(
                        src_ref=home_out.at[0, chip],
                        dst_ref=home_in.at[other, chip],
                        send_sem=home_send_sem.at[0, 0],
                        recv_sem=home_recv_sem.at[0, other],
                        device_id={"tok": sibling},
                        device_id_type=MESH,
                    ).wait_recv()
        half_heads = heads // 2
        start = half_heads * (top + group - 2 * top * group)
        for l in range(rounds):
            for place in range(half_heads):
                total = home_in[l, (start + place) * split]
                for p in range(1, split):
                    more = home_in[l, (start + place) * split + p]
                    total = (total.astype(F32) + more.astype(F32)).astype(BF16)
                grads[group, l * rows : (l + 1) * rows, parts[place]] = total

    def weight_gradient(group):
        with jax.named_scope(f"weight{group}"):
            normals = normal[...].reshape(rounds * rows, width)
            grad = dot_tn(normals, grads[group]) * grad_scale
            weights[group] = grad.astype(BF16).reshape(chips, width // chips, half_width)
            for copies in stages[0][group]:
                for mask in forwarding_order(copies):
                    copies[mask].start()

    def row_gradients(group):
        with jax.named_scope(f"rowgrad{group}"):
            columns = pl.ds(half_start(group), half_width)
            for l in range(rounds):
                part = dot_nt(grads[group, l * rows : (l + 1) * rows], maps[lane, :, columns])
                if group == 0:
                    rows_kept[l] = part
                else:
                    rows_kept[l] += part

    def run_sums(k, group):
        waiting = []
        with jax.named_scope(f"sum{k}_{group}"):
            for mask in forwarding_order(stages[k][group][0]):
                for place, (bit_order, columns) in enumerate(sections):
                    rest = mask - (1 << k)
                    sender = group if k < bits - 1 else 1 - group
                    stages[k][sender][place][mask].wait_recv()
                    slot = first_slot[k] + (mask >> (k + 1))
                    came = sums_in[group, slot, :, columns].astype(F32)
                    if k == 0:
                        row = flipped(chip, physical(bit_order, rest))
                        before = weights[group, row, :, columns]
                    else:
                        before = sums_run[group, rest >> 1, :, columns]
                    run = before.astype(F32) + came
                    if k == bits - 1:
                        column = pl.multiple_of(half_start(group) + columns.start, 128)
                        into = pl.ds(column, columns.stop - columns.start)
                        for l in range(rounds):
                            ends[l, :, into] = run[l * share : (l + 1) * share]
                        continue
                    sums_run[group, rest >> 1, :, columns] = run.astype(BF16)
                    waiting.append(stages[k + 1][group][place].get(rest))
                    if len(waiting) > 1:
                        onward = waiting.pop(0)
                        if onward is not None:
                            onward.start()
            for onward in waiting:
                if onward is not None:
                    onward.start()
            if k == bits - 1:
                end_copies[group].start()

    share = width // devices
    with jax.named_scope("ds"):
        looped(queries, 16, score_gradients)
    with jax.named_scope("dq"):
        looped(queries, 16, query_gradients)
    with jax.named_scope("dk"):
        looped(held, 16, key_gradients)
    with jax.named_scope("back"):
        looped(held, 16, bucket_back)
    send_home(1)
    normal_copy.wait_recv()
    assemble(0)
    weight_gradient(0)
    row_gradients(0)
    run_sums(0, 0)
    assemble(1)
    weight_gradient(1)
    for k in range(1, bits - 1):
        run_sums(k, 0)
    row_gradients(1)
    rows_out[...] = rows_kept[other].astype(BF16)
    rows_copy.start()
    for k in range(1, bits - 1):
        run_sums(k - 1, 1)
    rows_copy.wait_recv()
    d_normal = rows_kept[lane] + rows_in[...].astype(F32)
    with jax.named_scope("rows"):
        x = tokens_ref[...].astype(F32)
        scale = lax.rsqrt(jnp.mean(x * x, axis=-1, keepdims=True) + EPS)
        gain_total = jnp.sum(d_normal * (x * scale), axis=0, keepdims=True) * grad_scale
        share = width // devices
        gain_out[...] = jnp.zeros(gain_out.shape, F32)
        for device in range(devices):
            gain_out[device, 0:1, 0:share] = gain_total[:, device * share : (device + 1) * share]
        gain_back[me] = gain_out[me]
        for copy in gains:
            copy.start()
        t = d_normal * gain_ref[...]
        along = jnp.mean(x * t, axis=-1, keepdims=True)
        d_tokens_ref[...] = (t * scale - x * (scale * scale * scale * along)).astype(BF16)

    run_sums(bits - 2, 1)
    run_sums(bits - 1, 0)
    run_sums(bits - 1, 1)
    with jax.named_scope("ends"):
        d_weights_ref[lane] = ends[lane]
        for copy in end_copies:
            copy.wait_recv()
        d_weights_ref[other] = ends_in[...]
    with jax.named_scope("sendwaits"):
        for copy in gains:
            copy.wait_recv()
        d_gain_ref[...] = jnp.sum(gain_back[:, 0, :], axis=0, keepdims=True)
        for stage in stages:
            for copies in [*stage[0], *stage[1]]:
                for copy in copies.values():
                    copy.wait_send()
        for group in [*slabs, *relays, shares[-1]]:
            for copy in group.values():
                copy.wait_send()
        for t in range(2):
            for step in range(1, chips):
                homes[t][step].wait_send()
        pltpu.make_async_remote_copy(
            src_ref=home_out.at[0, chip],
            dst_ref=home_in.at[lane, chip],
            send_sem=home_send_sem.at[other, 0],
            recv_sem=home_recv_sem.at[0, lane],
            device_id={"tok": sibling},
            device_id_type=MESH,
        ).wait_send()
        for copy in [*row_sums, *gains, normal_copy, rows_copy, *end_copies]:
            copy.wait_send()


def hand_over(share, d_tokens_in, d_gain_in, d_weights_in, d_tokens, d_gain, d_qk, d_v, sems):
    pairs = [
        (d_tokens_in, d_tokens), (d_weights_in.at[1], d_qk), (d_weights_in.at[0], d_v)
    ]
    copies = [pltpu.make_async_copy(*pair, sems.at[i]) for i, pair in enumerate(pairs)]
    for copy in copies:
        copy.start()
    d_gain[...] = d_gain_in[:, :share]
    for copy in copies:
        copy.wait()


def per_device(tokens, norm_gain, w_qk, w_v, cotangent, log_sums, bucket_order, token_position):
    devices = lax.axis_size("tok")
    tok_dev, width = tokens.shape
    rounds, seq_len = bucket_order.shape
    heads = log_sums.shape[1]
    units = rounds * heads
    assert tok_dev == BLOCK and devices % units == 0 and rounds == 2
    split = devices // units
    chips = devices // rounds
    depth = width // heads
    queries = seq_len // tok_dev // split
    held = queries if split == 1 else queries + 1
    capacity = 5 * tok_dev // (4 * devices)
    stride = -(-capacity // 8) * 8
    grad_scale = 1.0 / math.sqrt(seq_len)
    share = width // devices
    dma = pltpu.SemaphoreType.DMA
    hbm, vmem = pl.ANY, pltpu.VMEM

    def low(*shape):
        return pltpu.VMEM(shape, BF16)

    def full(*shape):
        return pltpu.VMEM(shape, F32)

    results = pl.pallas_call(
        functools.partial(core_kernel, heads, stride, split, grad_scale),
        out_shape=[
            low(tok_dev, width),
            full(1, 128),
            full(2, share, width),
        ],
        in_specs=[pl.BlockSpec(memory_space=pl.ANY)] * 7,
        out_specs=whole(3),
        scratch_shapes=[
            full(1, width),
            pltpu.VMEM((rounds, seq_len), jnp.int32),
            full(rounds, heads, tok_dev),
            low(tok_dev, width),
            low(2, width, width),
            low(rounds, tok_dev, width),
            low(3, heads, tok_dev, depth),
            low(3, rounds, chips, tok_dev, depth),
            full(units, 1, tok_dev),
            full(devices, 1, tok_dev),
            low(devices, held, stride, tok_dev),
            low(held, devices * stride, tok_dev),
            low(devices, held, stride, depth),
            *[low(queries + 2, tok_dev, depth)] * 4,
            low(queries + 2, 2 * tok_dev, tok_dev),
            full(queries + 2, tok_dev, depth),
            low(rounds - 1, chips, tok_dev, depth),
            low(2, rounds - 1, chips, tok_dev, depth),
            *[low(2, chips, tok_dev, depth)] * 2,
            low(2, rounds * tok_dev, width // 2),
            full(rounds, tok_dev, width),
            *[low(tok_dev, width)] * 2,
            full(rounds, share, width),
            full(share, width),
            *[full(devices, 8, 128)] * 2,
            low(2, chips, width // chips, width // 2),
            low(2, chips - 1, width // chips, width // 2),
            low(2, chips // 2, width // chips, width // 2),
            dma((heads,)),
            dma((6,)),
            dma((3, chips - 1, 2)),
            dma((3, rounds - 1, chips, 2)),
            dma((devices - 1, 2)),
            dma((2, rounds - 1, chips, 2)),
            dma((2, chips)),
            dma((chips, rounds)),
            dma((devices - 1, 2)),
            dma((2, 2, chips - 1, 2)),
            dma((4, 2)),
        ],
        compiler_params=pltpu.CompilerParams(
            vmem_limit_bytes=VMEM_LIMIT, collective_id=0, has_side_effects=True
        ),
        name="core",
    )(norm_gain.reshape(1, width), bucket_order, log_sums, tokens, cotangent, w_qk, w_v)
    d_tokens, d_gain, d_qk, d_v = pl.pallas_call(
        functools.partial(hand_over, share),
        out_shape=[
            jax.ShapeDtypeStruct((tok_dev, width), BF16),
            jax.ShapeDtypeStruct((1, share), F32),
            jax.ShapeDtypeStruct((share, width), F32),
            jax.ShapeDtypeStruct((share, width), F32),
        ],
        in_specs=whole(3),
        out_specs=[pl.BlockSpec(memory_space=space) for space in (hbm, vmem, hbm, hbm)],
        scratch_shapes=[dma((3,))],
        name="hand_over",
    )(*[pltpu.with_memory_space_constraint(result, vmem) for result in results])
    return (d_tokens, d_gain.reshape(share), d_qk, d_v)


def solution(mesh):
    in_specs = (
        P(("groups", "tok"), None),
        P(),
        P(),
        P(),
        P(("groups", "tok"), None),
        P(None, None, ("groups", "tok")),
        P(None, "groups"),
        P(None, ("groups", "tok")),
    )
    out_specs = (
        P(("groups", "tok"), None),
        P(("groups", "tok")),
        P(("groups", "tok"), None),
        P(("groups", "tok"), None),
    )
    return jax.shard_map(
        per_device, mesh=mesh, in_specs=in_specs, out_specs=out_specs, check_vma=False
    )
```
